32 devices in a mesh: group: 2 (over x), lat: 16 (over z, y, core).
Axes of the slice: x: 2, y: 2, z: 4, core: 2. Of those that a mesh axis runs over, the one named last changes fastest.
Arguments:
- field: bfloat16 [1024, 512, 512], P(('group', 'lat')), parts along dimension 0, may hold values from -6 to 6
- lat_modes: float32 [64, 16, 16], replicated, may hold values from -1.5 to 1.5
- lat_gains: float32 [64, 16], replicated, may hold values from 2 to 16
- lat_local: float32 [16, 16], replicated, may hold values from -1.5 to 1.5
- depth_modes: float32 [16, 16, 16], replicated, may hold values from -1.5 to 1.5
- depth_local: float32 [16, 16], replicated, may hold values from -1.5 to 1.5
Outputs:
- result: bfloat16 [1024, 512, 512], P(('group', 'lat')), parts along dimension 0
The draws below stay inside these ranges and needn't reach their ends.
There are 2 independent parts, one for each index of `group`. The reference program is written for one: setup_inputs(seed, part) draws one part's arguments, and reference() takes and returns one part's arrays. A program takes and returns all parts, laid end to end along the dimension named above; an argument that names none is the same for every part. Nothing has to cross between parts.
All inputs are finite; a program needn't handle non-finite values.
Results may differ from the reference program's by a relative error of at most 0.001.
Values may be sent and summed in bfloat16 or wider, within the bound.
A program may use at most 192 MiB of HBM per device.

```python
import math
import jax
import jax.numpy as jnp
from jax import lax

X = 512
Y = 512
Z = 32
C = 16
KX = 64
KY = 64
KZ = 16
ZC = 512


def levels(rng, dims, pieces, smallest, top_value):
    factor_of, own = 1.0, jax.random.fold_in(rng, 6)
    for axis_at, parts in pieces:
        draws = jnp.exp(jax.random.uniform(jax.random.fold_in(own, axis_at), (parts,), jnp.float32, smallest / len(pieces), top_value / len(pieces)))
        factor_of = factor_of * jnp.repeat(draws, dims[axis_at] // parts).reshape([-1 if axis == axis_at else 1 for axis in range(len(dims))])
    return factor_of


def gaussian(rng, shape, deviation, most, shards=(), kind=jnp.bfloat16):
    values = deviation * jax.random.normal(rng, shape, jnp.float32)
    if shards:
        values = values * levels(rng, shape, shards, -0.22, 0.18)
    return jnp.clip(values, -most, most).astype(kind)


def setup_inputs(seed: int = 0, part: int = 0) -> dict:
    keys = jax.random.split(jax.random.key(seed), 7)
    part_splits = jax.random.split(jax.random.fold_in(keys[6], part), 7)
    field = gaussian(part_splits[0], (X, Y, ZC), 1.0, 6.0, ((0, 16),))
    lat_modes = gaussian(keys[1], (KX, C, C), C ** -0.5, 1.5, (), jnp.float32)
    lat_gains = jnp.clip(jnp.exp(jax.random.uniform(keys[2], (KY, C), jnp.float32, math.log(2.0), math.log(16.0))), 2.0, 16.0)
    lat_local = gaussian(keys[3], (C, C), C ** -0.5, 1.5, (), jnp.float32)
    depth_modes = gaussian(keys[4], (KZ, C, C), C ** -0.5, 1.5, (), jnp.float32)
    depth_local = gaussian(keys[5], (C, C), C ** -0.5, 1.5, (), jnp.float32)
    return {"field": field, "lat_modes": lat_modes, "lat_gains": lat_gains, "lat_local": lat_local, "depth_modes": depth_modes, "depth_local": depth_local}


def cosine_basis(length, modes):
    order = jnp.arange(modes, dtype=jnp.float32)[:, None]
    place = jnp.arange(length, dtype=jnp.float32)[None, :]
    scales = jnp.where(order == 0.0, math.sqrt(1.0 / length), math.sqrt(2.0 / length))
    return jnp.cos(math.pi * order * (place + 0.5) / length) * scales

def row_tail(u_rows, spect, lat_local, depth_modes, depth_local, depth_basis):
    highest = lax.Precision.HIGHEST
    rows, width, cells = u_rows.shape
    chans = lat_local.shape[0]
    depth = cells // chans
    u4 = u_rows.reshape(rows, width, depth, chans)
    s4 = spect.reshape(rows, width, depth, chans)
    first = u4 + jax.nn.gelu(s4 + jnp.einsum('xyzc,cd->xyzd', u4, lat_local, precision=highest))
    dcoef = jnp.einsum('kz,xyzc->xykc', depth_basis, first, precision=highest)
    dmix = jnp.einsum('xykc,kcd->xykd', dcoef, depth_modes, precision=highest)
    dspect = jnp.einsum('kz,xykd->xyzd', depth_basis, dmix, precision=highest)
    final = first + jax.nn.gelu(dspect + jnp.einsum('xyzc,cd->xyzd', first, depth_local, precision=highest))
    return final.reshape(rows, width, cells).astype(jnp.bfloat16)

def reference(field, lat_modes, lat_gains, lat_local, depth_modes, depth_local):
    highest = lax.Precision.HIGHEST
    basis_x = cosine_basis(X, KX)
    basis_y = cosine_basis(Y, KY)
    basis_z = cosine_basis(Z, KZ)
    block = min(X, 32)
    blocks = field.reshape(X // block, block, Y, Z * C)

    def forward_rows(rows):
        return jnp.einsum('qy,xyw->xqw', basis_y, rows.astype(jnp.float32), precision=highest)
    partial_coef = lax.map(forward_rows, blocks).reshape(X, KY, Z * C)
    coef = jnp.einsum('px,xqw->pqw', basis_x, partial_coef, precision=highest)
    coef4 = coef.reshape(KX, KY, Z, C) * lat_gains[None, :, None, :]
    mixed = jnp.einsum('pqzc,pcd->pqzd', coef4, lat_modes, precision=highest).reshape(KX, KY, Z * C)
    back_rows = jnp.einsum('px,pqw->xqw', basis_x, mixed, precision=highest)
    back_blocks = back_rows.reshape(X // block, block, KY, Z * C)

    def finish(pair):
        rows, back = pair
        spect = jnp.einsum('qy,xqw->xyw', basis_y, back, precision=highest)
        return row_tail(rows.astype(jnp.float32), spect, lat_local, depth_modes, depth_local, basis_z)
    out = lax.map(finish, (blocks, back_blocks))
    return out.reshape(X, Y, Z * C)
```

```python
import functools
import math

import jax
import jax.numpy as jnp
import numpy as np
from jax import lax
from jax.experimental import pallas as pl
from jax.experimental.pallas import tpu as pltpu
from jax.sharding import PartitionSpec as P

LINK = jnp.float16
SCALE_OUT = 256.0
SCALE_BACK = 1.0 / 16.0
K0 = math.sqrt(2.0 / math.pi)
K1 = K0 * 0.044715
MIB = 1 << 20


def cosine_basis(length, modes):
    order = np.arange(modes, dtype=np.float64)[:, None]
    place = np.arange(length, dtype=np.float64)[None, :]
    scales = np.where(order == 0.0, math.sqrt(1.0 / length), math.sqrt(2.0 / length))
    return (np.cos(math.pi * order * (place + 0.5) / length) * scales).astype(np.float32)


def halves(x):
    high = jnp.asarray(x).astype(jnp.bfloat16)
    low = (x - high.astype(jnp.float32)).astype(jnp.bfloat16)
    return high, low


def outer_halves(x):
    high = lax.reduce_precision(x, 8, 7)
    return high.astype(jnp.bfloat16), (x - high).astype(jnp.bfloat16)


def np_halves(x):
    high = np.asarray(x, dtype=jnp.bfloat16)
    low = np.asarray(x - high.astype(np.float32), dtype=jnp.bfloat16)
    return high, low


def dot(a, b):
    return jnp.dot(a, b, preferred_element_type=jnp.float32)


def gelu(x):
    half = 0.5 * x
    return half + half * jnp.tanh(x * (K0 + K1 * (x * x)))


def forward_kernel(basis_ref, u_ref, out_ref):
    modes = out_ref.shape[1]

    def body(row, carry):
        both = dot(basis_ref[...], u_ref[row])
        out_ref[row] = (both[:modes] + both[modes:]) * SCALE_OUT
        return carry

    lax.fori_loop(0, u_ref.shape[0], body, 0)


def forward(field, basis, start, rows):
    _, width, cells = field.shape
    modes = basis.shape[0] // 2
    step = math.gcd(rows, 4)
    return pl.pallas_call(
        forward_kernel,
        grid=(rows // step,),
        in_specs=[
            pl.BlockSpec(basis.shape, lambda i: (0, 0)),
            pl.BlockSpec((step, width, cells), lambda i: (i + start // step, 0, 0)),
        ],
        out_specs=pl.BlockSpec((step, modes, cells), lambda i: (i, 0, 0)),
        out_shape=jax.ShapeDtypeStruct((rows, modes, cells), jnp.float32),
        compiler_params=pltpu.CompilerParams(vmem_limit_bytes=40 * MIB),
        cost_estimate=pl.CostEstimate(
            flops=4 * rows * modes * width * cells,
            bytes_accessed=rows * cells * (2 * width + 4 * modes),
            transcendentals=0,
        ),
    )(basis, field)


def middle_kernel(chunks, chans, *refs):
    g_refs = refs[:chunks]
    f_refs = refs[chunks : 2 * chunks]
    b_refs = refs[2 * chunks : 3 * chunks]
    gain_ref, diag_ref = refs[3 * chunks : 3 * chunks + 2]
    out_refs = refs[3 * chunks + 2 :]
    modes = diag_ref.shape[1]
    coef = None
    for g_ref, f_ref in zip(g_refs, f_refs):
        high, low = halves(g_ref[0])
        both = dot(f_ref[...], high)
        part = both[:modes] + both[modes:] + dot(f_ref[:modes], low)
        coef = part if coef is None else coef + part
    coef = coef * gain_ref[0]
    tiles = []
    for lane in range(0, coef.shape[1], 128):
        tile = coef[:, lane : lane + 128]
        total = tile * diag_ref[chans - 1]
        for at in range(2 * chans - 1):
            shift = at - (chans - 1)
            if shift != 0:
                total += pltpu.roll(tile, (-shift) % 128, 1) * diag_ref[at]
        tiles.append(total)
    mixed = jnp.concatenate(tiles, axis=1) if len(tiles) > 1 else tiles[0]
    high, low = halves(mixed)
    stacked = jnp.concatenate([high, low, high], axis=0)
    for b_ref, out_ref in zip(b_refs, out_refs):
        out_ref[0] = dot(b_ref[...], stacked)


def middle(gathered, fronts, backs, gains, diags):
    chunks = len(gathered)
    count, length, width = gathered[0].shape
    modes = diags.shape[1]
    chans = (diags.shape[0] + 1) // 2
    whole = lambda a: pl.BlockSpec(a.shape, lambda i: (0,) * a.ndim)
    block = pl.BlockSpec((1, length, width), lambda i: (i, 0, 0))
    return pl.pallas_call(
        functools.partial(middle_kernel, chunks, chans),
        grid=(count,),
        in_specs=[block] * chunks
        + [whole(a) for a in fronts]
        + [whole(a) for a in backs]
        + [pl.BlockSpec((1, 1, width), lambda i: (i, 0, 0)), whole(diags)],
        out_specs=[block] * chunks,
        out_shape=[jax.ShapeDtypeStruct((count, length, width), jnp.float32)] * chunks,
        compiler_params=pltpu.CompilerParams(vmem_limit_bytes=40 * MIB),
    )(*gathered, *fronts, *backs, gains, diags)


def tail_kernel(piece, u_ref, back_ref, basis_ref, local_ref, depth_ref, *refs):
    out_ref = refs[-1]
    _, width, cells = u_ref.shape
    block = local_ref.shape[1]
    high, low = halves(back_ref[0])
    stacked = jnp.concatenate([high, low, high], axis=0)

    def body(at, carry):
        rows = pl.ds(pl.multiple_of(at * piece, piece), piece)
        u = u_ref[0, rows, :]
        spect = dot(basis_ref[rows, :], stacked)
        parts = []
        for lane in range(0, cells, block):
            tile = u[:, lane : lane + block]
            parts.append(dot(tile, local_ref[0]) + dot(tile, local_ref[1]))
        local = jnp.concatenate(parts, axis=1) if len(parts) > 1 else parts[0]
        first = u.astype(jnp.float32) + gelu(spect + local)
        high1, low1 = halves(first)
        mix = dot(high1, depth_ref[0]) + dot(low1, depth_ref[0]) + dot(high1, depth_ref[1])
        out_ref[0, rows, :] = (first + gelu(mix)).astype(out_ref.dtype)
        return carry

    lax.fori_loop(0, width // piece, body, 0)


def tail(field, back, basis, local, depth, previous, start):
    rows, modes, cells = back.shape
    width = field.shape[1]
    whole = lambda a: pl.BlockSpec(a.shape, lambda i: (0,) * a.ndim)
    operands = [field, back, basis, local, depth]
    specs = [
        pl.BlockSpec((1, width, cells), lambda i: (i + start, 0, 0)),
        pl.BlockSpec((1, modes, cells), lambda i: (i, 0, 0)),
        whole(basis),
        whole(local),
        whole(depth),
    ]
    aliases = {}
    if previous is not None:
        aliases = {len(operands): 0}
        operands.append(previous)
        specs.append(pl.BlockSpec(memory_space=pl.ANY))
    return pl.pallas_call(
        functools.partial(tail_kernel, math.gcd(width, 256)),
        grid=(rows,),
        in_specs=specs,
        out_specs=pl.BlockSpec((1, width, cells), lambda i: (i + start, 0, 0)),
        out_shape=jax.ShapeDtypeStruct(field.shape, jnp.bfloat16),
        input_output_aliases=aliases,
        compiler_params=pltpu.CompilerParams(vmem_limit_bytes=48 * MIB),
        cost_estimate=pl.CostEstimate(
            flops=2 * rows * width * cells * (4 * cells),
            bytes_accessed=4 * rows * width * cells,
            transcendentals=2 * rows * width * cells,
        ),
    )(*operands)


def block_diagonal(small, size):
    chans = small.shape[0]
    copies = size // chans
    ids = np.arange(size) // chans
    mask = (ids[:, None] == ids[None, :]).astype(np.float32)
    return jnp.tile(small, (copies, copies)) * mask


def shards_rows(field, lat_modes, lat_gains, lat_local, depth_modes, depth_local):
    highest = lax.Precision.HIGHEST
    devices = lax.axis_size("lat")
    rows_dev, width_y, cells = field.shape
    modes_x, chans, _ = lat_modes.shape
    modes_y = lat_gains.shape[0]
    modes_z = depth_modes.shape[0]
    depth = cells // chans
    width_x = rows_dev * devices
    chunks = 2 if rows_dev % 16 == 0 else 1
    rows = rows_dev // chunks
    splits = max(1, devices // modes_y)
    held = modes_y * splits // devices
    span = cells // splits
    basis_x = cosine_basis(width_x, modes_x)
    basis_y = cosine_basis(width_y, modes_y)
    basis_z = cosine_basis(depth, modes_z)

    high_y, low_y = np_halves(basis_y)
    front_y = jnp.asarray(np.concatenate([high_y, low_y], axis=0))
    back_y = jnp.asarray(np.concatenate([high_y, high_y, low_y], axis=0).T.copy())
    fronts, backs = [], []
    for chunk in range(chunks):
        part = basis_x.reshape(modes_x, devices, chunks, rows)[:, :, chunk].reshape(modes_x, -1)
        high_x, low_x = np_halves(part)
        fronts.append(jnp.asarray(np.concatenate([high_x, low_x], axis=0)))
        backs.append(jnp.asarray(np.concatenate([high_x, high_x, low_x], axis=0).T.copy()))

    gathered = []
    for chunk in range(chunks):
        coef_y = forward(field, front_y, chunk * rows, rows)
        sent = coef_y.astype(LINK).reshape(rows, modes_y, splits, span)
        sent = sent.transpose(1, 2, 0, 3).reshape(modes_y * splits, rows, span)
        gathered.append(lax.all_to_all(sent, "lat", split_axis=0, concat_axis=0, tiled=True))

    shift = np.arange(2 * chans - 1)[:, None, None] - (chans - 1)
    places = np.arange(chans)
    pick = (places[None, :, None] == places[None, None, :] + shift).astype(np.float32)
    diags = jnp.sum(lat_modes[None] * pick[:, None], axis=2)
    diags = jnp.tile(diags, (1, 1, 128 // chans))
    me = lax.axis_index("lat")
    gain_rows = lax.dynamic_slice_in_dim(lat_gains, me * held // splits, held, 0)
    gain_rows = jnp.tile(gain_rows * (SCALE_BACK / SCALE_OUT), (1, span // chans))[:, None, :]

    spread = np.kron(basis_z.T, np.eye(chans, dtype=np.float32))
    ids = np.arange(modes_z * chans) // chans
    mask = (ids[:, None] == ids[None, :]).astype(np.float32)
    mixers = jnp.tile(depth_modes.reshape(modes_z * chans, chans), (1, modes_z)) * mask
    inner = jnp.dot(mixers, spread.T, precision=highest)
    whole = jnp.dot(spread, inner, precision=highest) + block_diagonal(depth_local, cells)
    depth_pair = jnp.stack(outer_halves(whole))
    local_pair = jnp.stack(outer_halves(block_diagonal(lat_local, math.gcd(cells, 256))))

    received = []
    for got in gathered:
        got = got.reshape(devices, held, rows, span).transpose(1, 0, 2, 3).astype(jnp.float32)
        received.append(got.reshape(held, devices * rows, span))
    mixed = middle(received, fronts, backs, gain_rows, diags)
    returned = []
    for part in mixed:
        part = part.astype(LINK).reshape(held, devices, rows, span).transpose(1, 0, 2, 3)
        part = part.reshape(devices * held, rows, span)
        returned.append(lax.all_to_all(part, "lat", split_axis=0, concat_axis=0, tiled=True))
    out = None
    for chunk, part in enumerate(returned):
        part = part.reshape(modes_y, splits, rows, span).transpose(2, 0, 1, 3)
        part = part.reshape(rows, modes_y, cells).astype(jnp.float32) * (1.0 / SCALE_BACK)
        out = tail(field, part, back_y, local_pair, depth_pair, out, chunk * rows)
    return out

LINK_OUT = 64.0
LINK_BACK = 1.0 / 32.0
C0 = 2.0 * K0
C1 = 8.0 * K1


def act(h):
    return h + h * jnp.tanh(h * (C0 + C1 * (h * h)))


def window_factors(basis, windows, fine):
    modes = basis.shape[0]
    blocks = basis.reshape(modes, windows, -1).transpose(1, 0, 2)
    left, sizes, right = np.linalg.svd(blocks, full_matrices=False)
    left = left * sizes[:, None, :]
    top = np.abs(basis).max()
    rank = fine
    while rank < sizes.shape[1]:
        product = left[:, :, :rank] @ right[:, :rank]
        if np.abs(product - blocks).max() <= 2.0 ** -25 * top:
            break
        rank += fine
    return left[:, :, :rank], right[:, :rank]


def analysis_kernel(me_ref, basis_ref, press_ref, u_ref, out_ref, high_ref, low_ref):
    step, modes, cells = u_ref.shape[0], basis_ref.shape[0] // 2, u_ref.shape[2]
    at = pl.program_id(0)
    for row in range(step):
        both = dot(basis_ref[...], u_ref[row])
        high, low = halves(both[:modes] + both[modes:])
        high_ref[at * step + row] = high
        low_ref[at * step + row] = low

    @pl.when(at == pl.num_programs(0) - 1)
    def _():
        count = press_ref.shape[1]
        rows = high_ref.shape[0]
        for group in range(modes // 16):
            take = slice(16 * group, 16 * group + 16)
            high = high_ref[:, take, :].reshape(rows * 16, cells)
            low = low_ref[:, take, :].reshape(rows * 16, cells)
            stacked = jnp.concatenate([high, low, high], axis=0)
            out_ref[count * group : count * (group + 1), :] = dot(press_ref[0], stacked)


def analysis(field, basis, press, me):
    rows, width, cells = field.shape
    modes = basis.shape[0] // 2
    step = math.gcd(rows, 4)
    out_rows = modes // 16 * press.shape[1]
    return pl.pallas_call(
        analysis_kernel,
        grid_spec=pltpu.PrefetchScalarGridSpec(
            num_scalar_prefetch=1,
            grid=(rows // step,),
            in_specs=[
                pl.BlockSpec(basis.shape, lambda i, me: (0, 0)),
                pl.BlockSpec((1,) + press.shape[1:], lambda i, me: (me[0], 0, 0)),
                pl.BlockSpec((step, width, cells), lambda i, me: (i, 0, 0)),
            ],
            out_specs=pl.BlockSpec((out_rows, cells), lambda i, me: (0, 0)),
            scratch_shapes=[pltpu.VMEM((rows, modes, cells), jnp.bfloat16)] * 2,
        ),
        out_shape=jax.ShapeDtypeStruct((out_rows, cells), jnp.float32),
        compiler_params=pltpu.CompilerParams(vmem_limit_bytes=48 * MIB),
    )(me, basis, press, field)


def swap(blocks, devices):
    groups = [list(range(core, devices, 2)) for core in range(2)]
    return lax.all_to_all(blocks, "lat", split_axis=0, concat_axis=0, axis_index_groups=groups, tiled=True)


def turn(x, unit):
    place = lax.broadcasted_iota(jnp.int32, (x.shape[0], 128), 1)
    place = (128 - unit - place // unit * unit) + place % unit
    tiles = [jnp.take_along_axis(x[:, at : at + 128], place, axis=1) for at in range(0, x.shape[1], 128)]
    return jnp.concatenate(tiles[::-1], axis=1)


def blend_kernel(chans, c_ref, front_ref, back_ref, gain_ref, diag_ref, out_ref):
    modes = diag_ref.shape[1]
    held = gain_ref.shape[0]
    high, low = halves(c_ref[...])
    coef = dot(front_ref[...], jnp.concatenate([high, low, high], axis=0))
    highs, lows = [], []
    for q in range(held):
        part = coef[q * modes : (q + 1) * modes] * gain_ref[q]
        tiles = []
        for lane in range(0, part.shape[1], 128):
            tile = part[:, lane : lane + 128]
            total = tile * diag_ref[chans - 1]
            for at in range(2 * chans - 1):
                shift = at - (chans - 1)
                if shift != 0:
                    total += pltpu.roll(tile, (-shift) % 128, 1) * diag_ref[at]
            tiles.append(total)
        mixed = jnp.concatenate(tiles, axis=1)
        half = mixed.shape[1] // 2
        mixed = jnp.concatenate([mixed[:, :half], turn(mixed[:, half:], chans)], axis=1)
        high, low = halves(mixed)
        highs.append(high)
        lows.append(low)
    out_ref[...] = dot(back_ref[...], jnp.concatenate(highs + lows + highs, axis=0))


def blend(coefs, front, back, gains, diags, chans):
    whole = lambda a: pl.BlockSpec(a.shape, lambda: (0,) * a.ndim)
    args = (coefs, front, back, gains, diags)
    return pl.pallas_call(
        functools.partial(blend_kernel, chans),
        in_specs=[whole(a) for a in args],
        out_specs=whole(coefs),
        out_shape=jax.ShapeDtypeStruct(coefs.shape, jnp.float32),
        compiler_params=pltpu.CompilerParams(vmem_limit_bytes=40 * MIB),
    )(*args)


def finish_kernel(chans, me_ref, u_ref, c_ref, grow_ref, basis_ref, local_ref, depth_ref, out_ref, high_ref, low_ref, *rhs):
    rows, width, cells = u_ref.shape
    half = cells // 2
    modes = high_ref.shape[1]
    at = pl.program_id(0)

    @pl.when(at == 0)
    def _():
        total = high_ref.shape[0]
        count = grow_ref.shape[2] // 3
        for group in range(modes // 16):
            high, low = halves(c_ref[count * group : count * (group + 1), :])
            back = dot(grow_ref[0], jnp.concatenate([high, low, high], axis=0))
            high, low = halves(back)
            take = slice(16 * group, 16 * group + 16)
            high_ref[:, take, :] = high.reshape(total, 16, cells)
            low_ref[:, take, :] = low.reshape(total, 16, cells)
        for r in rhs:
            r[:, 4 * modes :, :] = local_ref[...]

    def first_layer(row):
        high, low = high_ref[at * rows + row], low_ref[at * rows + row]
        parts = []
        for side in range(2):
            lanes = slice(side * half, (side + 1) * half)
            for k, x in enumerate((high, low, high, low)):
                rhs[row][side, modes * k : modes * (k + 1), :] = x[:, lanes]
            u = u_ref[row, :, lanes]
            h = dot(jnp.concatenate([basis_ref[...], u, u], axis=1), rhs[row][side])
            wide = u.astype(jnp.float32)
            parts.append((turn(wide, chans) if side else wide) + act(h))
        return parts

    def second_layer(row, first):
        mixes = []
        for side, x in enumerate((first[0] + first[1], first[0] - first[1])):
            high, low = halves(x)
            mixes.append(dot(jnp.concatenate([high, low, high], axis=1), depth_ref[side]))
        upper = first[1] + act(mixes[0] - mixes[1])
        out_ref[row, :, :half] = (first[0] + act(mixes[0] + mixes[1])).astype(out_ref.dtype)
        out_ref[row, :, half:] = turn(upper, chans).astype(out_ref.dtype)

    firsts = [first_layer(0)]
    for row in range(rows):
        if row + 1 < rows:
            firsts.append(first_layer(row + 1))
        second_layer(row, firsts[row])


def finish(field, coefs, grow, basis, local, depth, me, chans):
    rows, width, cells = field.shape
    modes = basis.shape[1] // 4
    step = math.gcd(rows, 2)
    whole = lambda a: pl.BlockSpec(a.shape, lambda i, me: (0,) * a.ndim)
    return pl.pallas_call(
        functools.partial(finish_kernel, chans),
        grid_spec=pltpu.PrefetchScalarGridSpec(
            num_scalar_prefetch=1,
            grid=(rows // step,),
            in_specs=[
                pl.BlockSpec((step, width, cells), lambda i, me: (i, 0, 0)),
                whole(coefs),
                pl.BlockSpec((1,) + grow.shape[1:], lambda i, me: (me[0], 0, 0)),
                whole(basis),
                whole(local),
                whole(depth),
            ],
            out_specs=pl.BlockSpec((step, width, cells), lambda i, me: (i, 0, 0)),
            scratch_shapes=[pltpu.VMEM((rows, modes, cells), jnp.bfloat16)] * 2
            + [pltpu.VMEM((2, 4 * modes + cells, cells // 2), jnp.bfloat16)] * step,
        ),
        out_shape=jax.ShapeDtypeStruct(field.shape, jnp.bfloat16),
        compiler_params=pltpu.CompilerParams(vmem_limit_bytes=56 * MIB),
        cost_estimate=pl.CostEstimate(
            flops=2 * rows * width * cells * (3 * cells),
            bytes_accessed=4 * rows * width * cells,
            transcendentals=2 * rows * width * cells,
        ),
    )(me, field, coefs, grow, basis, local, depth)


def stack_halves(x, order, axis):
    pair = np_halves(np.asarray(x, dtype=np.float32))
    return np.concatenate([pair[k] for k in order], axis=axis)


def shards_chips(devices, field, lat_modes, lat_gains, lat_local, depth_modes, depth_local):
    highest = lax.Precision.HIGHEST
    rows, width_y, cells = field.shape
    modes_x, chans, _ = lat_modes.shape
    modes_y = lat_gains.shape[0]
    modes_z = depth_modes.shape[0]
    depth = cells // chans
    chips = devices // 2
    held = modes_y // devices
    basis_y = cosine_basis(width_y, modes_y)
    basis_z = cosine_basis(depth, modes_z)
    left, right = window_factors(wide_basis(rows * devices, modes_x), chips, 8 // math.gcd(held, 8))
    rank = left.shape[2]
    me = lax.axis_index("lat")
    at = me.reshape(1)

    own = right.reshape(chips, rank, 2, rows).transpose(0, 2, 1, 3).reshape(devices, rank, rows)
    eye = np.eye(16)
    press = np.einsum("djx,qr->dqjxr", own * LINK_OUT, eye).reshape(devices, 16 * rank, rows * 16)
    press = jnp.asarray(stack_halves(press, (0, 0, 1), 2))
    grow = np.einsum("djx,qr->dxqrj", own * (0.5 / LINK_BACK), eye).reshape(devices, rows * 16, 16 * rank)
    grow = jnp.asarray(stack_halves(grow, (0, 0, 1), 2))
    sides = np.einsum("ipj,qr->qpirj", left, np.eye(held)).reshape(held * modes_x, chips * held * rank)
    front = jnp.asarray(stack_halves(sides, (0, 0, 1), 1))
    back = jnp.asarray(stack_halves(sides.T, (0, 0, 1), 1))
    front_y = jnp.asarray(stack_halves(basis_y, (0, 1), 0))
    back_y = jnp.asarray(stack_halves(basis_y.T, (0, 0, 1, 1), 1))

    partial = analysis(field, front_y, press, at).reshape(2, modes_y // 2 * rank, cells)
    core = lax.rem(me, 2)
    keep = lax.dynamic_index_in_dim(partial, core, 0, keepdims=False)
    give = lax.dynamic_index_in_dim(partial, 1 - core, 0, keepdims=False)
    got = lax.ppermute(give, "lat", [(d, d ^ 1) for d in range(devices)])
    sent = (keep + got).astype(LINK).reshape(chips, held * rank, cells)

    shift = np.arange(2 * chans - 1)[:, None, None] - (chans - 1)
    places = np.arange(chans)
    pick = (places[None, :, None] == places[None, None, :] + shift).astype(np.float32)
    diags = jnp.sum(lat_modes[None] * pick[:, None], axis=2)
    diags = jnp.tile(diags, (1, 1, 128 // chans))
    first_q = core * (modes_y // 2) + me // 2 * held
    gains = lax.dynamic_slice_in_dim(lat_gains, first_q, held, 0) * (LINK_BACK / LINK_OUT)
    gains = jnp.tile(gains, (1, depth))[:, None, :]

    folds, mixers = [], []
    half = depth // 2
    ids = np.arange(modes_z // 2 * chans) // chans
    mask = (ids[:, None] == ids[None, :]).astype(np.float32)
    for side in range(2):
        folds.append(np.kron(basis_z[side::2, :half].T, np.eye(chans, dtype=np.float32)))
        mixers.append(jnp.tile(depth_modes[side::2].reshape(modes_z // 2 * chans, chans), (1, modes_z // 2)) * mask)
    folds = np.stack(folds)
    inner = jnp.einsum("skm,snm->skn", jnp.stack(mixers), folds, precision=highest)
    whole = jnp.einsum("snk,skm->snm", 0.5 * folds, inner, precision=highest)
    whole = whole + 0.25 * block_diagonal(depth_local, cells // 2)[None]
    high, low = outer_halves(whole)
    depth_ops = jnp.concatenate([high, high, low], axis=1)

    ids = np.arange(cells // 2) // chans
    tiled = jnp.tile(0.5 * lat_local, (half, half))
    straight = tiled * (ids[:, None] == ids[None, :]).astype(np.float32)
    turned = tiled * (ids[:, None] == half - 1 - ids[None, :]).astype(np.float32)
    high, low = outer_halves(jnp.stack([straight, turned]))
    local_ops = jnp.concatenate([high, low], axis=1)

    gathered = swap(sent, devices).astype(jnp.float32).reshape(chips * held * rank, cells)
    mixed = blend(gathered, front, back, gains, diags, chans)
    mine = swap(mixed.astype(LINK).reshape(chips, held * rank, cells), devices)
    theirs = lax.ppermute(mine, "lat", [(d, d ^ 1) for d in range(devices)])
    first = core == 0
    pair = jnp.stack([jnp.where(first, mine, theirs), jnp.where(first, theirs, mine)])
    coefs = pair.astype(jnp.float32).reshape(modes_y * rank, cells)
    return finish(field, coefs, grow, back_y, local_ops, depth_ops, at, chans)


def wide_basis(length, modes):
    order = np.arange(modes, dtype=np.float64)[:, None]
    place = np.arange(length, dtype=np.float64)[None, :]
    scales = np.where(order == 0.0, math.sqrt(1.0 / length), math.sqrt(2.0 / length))
    return np.cos(math.pi * order * (place + 0.5) / length) * scales


def shards(field, lat_modes, lat_gains, lat_local, depth_modes, depth_local):
    devices = lax.axis_size("lat")
    rows, _, cells = field.shape
    chans = lat_local.shape[0]
    modes_y, modes_z = lat_gains.shape[0], depth_modes.shape[0]
    fits = devices % 2 == 0 and modes_y % max(devices, 16) == 0 and rows % 4 == 0
    fits = fits and modes_z % 2 == 0 and cells % 256 == 0 and cells // chans % 2 == 0
    args = (field, lat_modes, lat_gains, lat_local, depth_modes, depth_local)
    return shards_chips(devices, *args) if fits else shards_rows(*args)


def solution(mesh):
    placed = (P(("group", "lat"), None, None), P(), P(), P(), P(), P())
    return jax.shard_map(
        shards,
        mesh=mesh,
        in_specs=placed,
        out_specs=P(("group", "lat"), None, None),
        check_vma=False,
    )
```

```python
import functools
import math

import jax
import jax.numpy as jnp
import numpy as np
from jax import lax
from jax.experimental import pallas as pl
from jax.experimental.pallas import tpu as pltpu
from jax.sharding import PartitionSpec as P

LINK = jnp.float16
SCALE_OUT = 256.0
SCALE_BACK = 1.0 / 16.0
K0 = math.sqrt(2.0 / math.pi)
K1 = K0 * 0.044715
MIB = 1 << 20


def cosine_basis(length, modes):
    order = np.arange(modes, dtype=np.float64)[:, None]
    place = np.arange(length, dtype=np.float64)[None, :]
    scales = np.where(order == 0.0, math.sqrt(1.0 / length), math.sqrt(2.0 / length))
    return (np.cos(math.pi * order * (place + 0.5) / length) * scales).astype(np.float32)


def halves(x):
    high = jnp.asarray(x).astype(jnp.bfloat16)
    low = (x - high.astype(jnp.float32)).astype(jnp.bfloat16)
    return high, low


def outer_halves(x):
    high = lax.reduce_precision(x, 8, 7)
    return high.astype(jnp.bfloat16), (x - high).astype(jnp.bfloat16)


def np_halves(x):
    high = np.asarray(x, dtype=jnp.bfloat16)
    low = np.asarray(x - high.astype(np.float32), dtype=jnp.bfloat16)
    return high, low


def dot(a, b):
    return jnp.dot(a, b, preferred_element_type=jnp.float32)


def gelu(x):
    half = 0.5 * x
    return half + half * jnp.tanh(x * (K0 + K1 * (x * x)))


def forward_kernel(basis_ref, u_ref, out_ref):
    modes = out_ref.shape[1]

    def body(row, carry):
        both = dot(basis_ref[...], u_ref[row])
        out_ref[row] = (both[:modes] + both[modes:]) * SCALE_OUT
        return carry

    lax.fori_loop(0, u_ref.shape[0], body, 0)


def forward(field, basis, start, rows):
    _, width, cells = field.shape
    modes = basis.shape[0] // 2
    step = math.gcd(rows, 4)
    return pl.pallas_call(
        forward_kernel,
        grid=(rows // step,),
        in_specs=[
            pl.BlockSpec(basis.shape, lambda i: (0, 0)),
            pl.BlockSpec((step, width, cells), lambda i: (i + start // step, 0, 0)),
        ],
        out_specs=pl.BlockSpec((step, modes, cells), lambda i: (i, 0, 0)),
        out_shape=jax.ShapeDtypeStruct((rows, modes, cells), jnp.float32),
        compiler_params=pltpu.CompilerParams(vmem_limit_bytes=40 * MIB),
        cost_estimate=pl.CostEstimate(
            flops=4 * rows * modes * width * cells,
            bytes_accessed=rows * cells * (2 * width + 4 * modes),
            transcendentals=0,
        ),
    )(basis, field)


def middle_kernel(chunks, chans, *refs):
    g_refs = refs[:chunks]
    f_refs = refs[chunks : 2 * chunks]
    b_refs = refs[2 * chunks : 3 * chunks]
    gain_ref, diag_ref = refs[3 * chunks : 3 * chunks + 2]
    out_refs = refs[3 * chunks + 2 :]
    modes = diag_ref.shape[1]
    coef = None
    for g_ref, f_ref in zip(g_refs, f_refs):
        high, low = halves(g_ref[0])
        both = dot(f_ref[...], high)
        part = both[:modes] + both[modes:] + dot(f_ref[:modes], low)
        coef = part if coef is None else coef + part
    coef = coef * gain_ref[0]
    tiles = []
    for lane in range(0, coef.shape[1], 128):
        tile = coef[:, lane : lane + 128]
        total = tile * diag_ref[chans - 1]
        for at in range(2 * chans - 1):
            shift = at - (chans - 1)
            if shift != 0:
                total += pltpu.roll(tile, (-shift) % 128, 1) * diag_ref[at]
        tiles.append(total)
    mixed = jnp.concatenate(tiles, axis=1) if len(tiles) > 1 else tiles[0]
    high, low = halves(mixed)
    stacked = jnp.concatenate([high, low, high], axis=0)
    for b_ref, out_ref in zip(b_refs, out_refs):
        out_ref[0] = dot(b_ref[...], stacked)


def middle(gathered, fronts, backs, gains, diags):
    chunks = len(gathered)
    count, length, width = gathered[0].shape
    modes = diags.shape[1]
    chans = (diags.shape[0] + 1) // 2
    whole = lambda a: pl.BlockSpec(a.shape, lambda i: (0,) * a.ndim)
    block = pl.BlockSpec((1, length, width), lambda i: (i, 0, 0))
    return pl.pallas_call(
        functools.partial(middle_kernel, chunks, chans),
        grid=(count,),
        in_specs=[block] * chunks
        + [whole(a) for a in fronts]
        + [whole(a) for a in backs]
        + [pl.BlockSpec((1, 1, width), lambda i: (i, 0, 0)), whole(diags)],
        out_specs=[block] * chunks,
        out_shape=[jax.ShapeDtypeStruct((count, length, width), jnp.float32)] * chunks,
        compiler_params=pltpu.CompilerParams(vmem_limit_bytes=40 * MIB),
    )(*gathered, *fronts, *backs, gains, diags)


def tail_kernel(piece, u_ref, back_ref, basis_ref, local_ref, depth_ref, *refs):
    out_ref = refs[-1]
    _, width, cells = u_ref.shape
    block = local_ref.shape[1]
    high, low = halves(back_ref[0])
    stacked = jnp.concatenate([high, low, high], axis=0)

    def body(at, carry):
        rows = pl.ds(pl.multiple_of(at * piece, piece), piece)
        u = u_ref[0, rows, :]
        spect = dot(basis_ref[rows, :], stacked)
        parts = []
        for lane in range(0, cells, block):
            tile = u[:, lane : lane + block]
            parts.append(dot(tile, local_ref[0]) + dot(tile, local_ref[1]))
        local = jnp.concatenate(parts, axis=1) if len(parts) > 1 else parts[0]
        first = u.astype(jnp.float32) + gelu(spect + local)
        high1, low1 = halves(first)
        mix = dot(high1, depth_ref[0]) + dot(low1, depth_ref[0]) + dot(high1, depth_ref[1])
        out_ref[0, rows, :] = (first + gelu(mix)).astype(out_ref.dtype)
        return carry

    lax.fori_loop(0, width // piece, body, 0)


def tail(field, back, basis, local, depth, previous, start):
    rows, modes, cells = back.shape
    width = field.shape[1]
    whole = lambda a: pl.BlockSpec(a.shape, lambda i: (0,) * a.ndim)
    operands = [field, back, basis, local, depth]
    specs = [
        pl.BlockSpec((1, width, cells), lambda i: (i + start, 0, 0)),
        pl.BlockSpec((1, modes, cells), lambda i: (i, 0, 0)),
        whole(basis),
        whole(local),
        whole(depth),
    ]
    aliases = {}
    if previous is not None:
        aliases = {len(operands): 0}
        operands.append(previous)
        specs.append(pl.BlockSpec(memory_space=pl.ANY))
    return pl.pallas_call(
        functools.partial(tail_kernel, math.gcd(width, 256)),
        grid=(rows,),
        in_specs=specs,
        out_specs=pl.BlockSpec((1, width, cells), lambda i: (i + start, 0, 0)),
        out_shape=jax.ShapeDtypeStruct(field.shape, jnp.bfloat16),
        input_output_aliases=aliases,
        compiler_params=pltpu.CompilerParams(vmem_limit_bytes=48 * MIB),
        cost_estimate=pl.CostEstimate(
            flops=2 * rows * width * cells * (4 * cells),
            bytes_accessed=4 * rows * width * cells,
            transcendentals=2 * rows * width * cells,
        ),
    )(*operands)


def block_diagonal(small, size):
    chans = small.shape[0]
    copies = size // chans
    ids = np.arange(size) // chans
    mask = (ids[:, None] == ids[None, :]).astype(np.float32)
    return jnp.tile(small, (copies, copies)) * mask


def shards_rows(field, lat_modes, lat_gains, lat_local, depth_modes, depth_local):
    highest = lax.Precision.HIGHEST
    devices = lax.axis_size("lat")
    rows_dev, width_y, cells = field.shape
    modes_x, chans, _ = lat_modes.shape
    modes_y = lat_gains.shape[0]
    modes_z = depth_modes.shape[0]
    depth = cells // chans
    width_x = rows_dev * devices
    chunks = 2 if rows_dev % 16 == 0 else 1
    rows = rows_dev // chunks
    splits = max(1, devices // modes_y)
    held = modes_y * splits // devices
    span = cells // splits
    basis_x = cosine_basis(width_x, modes_x)
    basis_y = cosine_basis(width_y, modes_y)
    basis_z = cosine_basis(depth, modes_z)

    high_y, low_y = np_halves(basis_y)
    front_y = jnp.asarray(np.concatenate([high_y, low_y], axis=0))
    back_y = jnp.asarray(np.concatenate([high_y, high_y, low_y], axis=0).T.copy())
    fronts, backs = [], []
    for chunk in range(chunks):
        part = basis_x.reshape(modes_x, devices, chunks, rows)[:, :, chunk].reshape(modes_x, -1)
        high_x, low_x = np_halves(part)
        fronts.append(jnp.asarray(np.concatenate([high_x, low_x], axis=0)))
        backs.append(jnp.asarray(np.concatenate([high_x, high_x, low_x], axis=0).T.copy()))

    gathered = []
    for chunk in range(chunks):
        coef_y = forward(field, front_y, chunk * rows, rows)
        sent = coef_y.astype(LINK).reshape(rows, modes_y, splits, span)
        sent = sent.transpose(1, 2, 0, 3).reshape(modes_y * splits, rows, span)
        gathered.append(lax.all_to_all(sent, "lat", split_axis=0, concat_axis=0, tiled=True))

    shift = np.arange(2 * chans - 1)[:, None, None] - (chans - 1)
    places = np.arange(chans)
    pick = (places[None, :, None] == places[None, None, :] + shift).astype(np.float32)
    diags = jnp.sum(lat_modes[None] * pick[:, None], axis=2)
    diags = jnp.tile(diags, (1, 1, 128 // chans))
    me = lax.axis_index("lat")
    gain_rows = lax.dynamic_slice_in_dim(lat_gains, me * held // splits, held, 0)
    gain_rows = jnp.tile(gain_rows * (SCALE_BACK / SCALE_OUT), (1, span // chans))[:, None, :]

    spread = np.kron(basis_z.T, np.eye(chans, dtype=np.float32))
    ids = np.arange(modes_z * chans) // chans
    mask = (ids[:, None] == ids[None, :]).astype(np.float32)
    mixers = jnp.tile(depth_modes.reshape(modes_z * chans, chans), (1, modes_z)) * mask
    inner = jnp.dot(mixers, spread.T, precision=highest)
    whole = jnp.dot(spread, inner, precision=highest) + block_diagonal(depth_local, cells)
    depth_pair = jnp.stack(outer_halves(whole))
    local_pair = jnp.stack(outer_halves(block_diagonal(lat_local, math.gcd(cells, 256))))

    received = []
    for got in gathered:
        got = got.reshape(devices, held, rows, span).transpose(1, 0, 2, 3).astype(jnp.float32)
        received.append(got.reshape(held, devices * rows, span))
    mixed = middle(received, fronts, backs, gain_rows, diags)
    returned = []
    for part in mixed:
        part = part.astype(LINK).reshape(held, devices, rows, span).transpose(1, 0, 2, 3)
        part = part.reshape(devices * held, rows, span)
        returned.append(lax.all_to_all(part, "lat", split_axis=0, concat_axis=0, tiled=True))
    out = None
    for chunk, part in enumerate(returned):
        part = part.reshape(modes_y, splits, rows, span).transpose(2, 0, 1, 3)
        part = part.reshape(rows, modes_y, cells).astype(jnp.float32) * (1.0 / SCALE_BACK)
        out = tail(field, part, back_y, local_pair, depth_pair, out, chunk * rows)
    return out

LINK_OUT = 64.0
LINK_BACK = 1.0 / 32.0
C0 = 2.0 * K0
C1 = 8.0 * K1


def act(h):
    return h + h * jnp.tanh(h * (C0 + C1 * (h * h)))


def window_factors(basis, windows, fine):
    modes = basis.shape[0]
    blocks = basis.reshape(modes, windows, -1).transpose(1, 0, 2)
    left, sizes, right = np.linalg.svd(blocks, full_matrices=False)
    left = left * sizes[:, None, :]
    top = np.abs(basis).max()
    rank = fine
    while rank < sizes.shape[1]:
        product = left[:, :, :rank] @ right[:, :rank]
        if np.abs(product - blocks).max() <= 2.0 ** -25 * top:
            break
        rank += fine
    return left[:, :, :rank], right[:, :rank]


def turn(x, unit):
    place = lax.broadcasted_iota(jnp.int32, (x.shape[0], 128), 1)
    place = (128 - unit - place // unit * unit) + place % unit
    tiles = [jnp.take_along_axis(x[:, at : at + 128], place, axis=1) for at in range(0, x.shape[1], 128)]
    return jnp.concatenate(tiles[::-1], axis=1)


LEAD = 8
CHUNK = 128


def exact(a, b):
    return jnp.dot(a, b, preferred_element_type=jnp.float32, precision=lax.Precision.HIGHEST)


def block_mask(size, unit, flip):
    row = lax.broadcasted_iota(jnp.int32, (size, size), 0) // unit
    lane = lax.broadcasted_iota(jnp.int32, (size, size), 1) // unit
    return (row == (size // unit - 1 - lane if flip else lane)).astype(jnp.float32)


def exchange_kernel(chips, held, rank, chans, *refs):
    (field, press_all, grow_all, basis, front, back, gains, modes_in, picks, folds, folds_t, sides, spread8, spread16, spread_t, depth_in,
     depth_local, lat_local, high_out, low_out, depth_out, local_out) = refs[:22]
    (u, press, grow, highs, lows, part, fresh, send, land, reply, home, wide_high, wide_low, diags, depth_ops, local_ops) = refs[22:38]
    load_sem, table_sem, pair_send, pair_recv, out_send, out_recv, in_send, in_recv, hand_send, hand_recv, store_sem, ops_sem = refs[38:]
    rows, width, cells = field.shape
    modes = basis.shape[0] // 2
    chunks = cells // CHUNK
    tall, lead = held * rank, held * LEAD
    mesh_ids = pl.DeviceIdType.MESH
    me = lax.axis_index("lat")
    chip, core = me // 2, lax.rem(me, 2)
    other = chip * 2 + 1 - core
    subs = 4
    span = rows // subs

    def load(ch, sub):
        take = pl.ds(sub * span, span)
        return pltpu.make_async_copy(
            field.at[take, :, pl.ds(ch * CHUNK, CHUNK)], u.at[ch % 2, take], load_sem.at[ch, sub]
        )

    def tables():
        return (
            pltpu.make_async_copy(press_all.at[me], press, table_sem.at[0]),
            pltpu.make_async_copy(grow_all.at[me], grow, table_sem.at[1]),
        )

    for sub in range(subs):
        load(0, sub).start()
    for copy in tables():
        copy.start()
    for sub in range(subs):
        load(1, sub).start()

    barrier = pltpu.get_barrier_semaphore()
    for off in range(1, chips):
        peer = lax.rem(chip + off, chips) * 2 + core
        pl.semaphore_signal(barrier, inc=1, device_id={"lat": peer}, device_id_type=mesh_ids)
    pl.semaphore_signal(barrier, inc=1, device_id={"lat": other}, device_id_type=mesh_ids)

    def pair_copy(ch):
        return pltpu.make_async_remote_copy(
            src_ref=part.at[ch, 1 - core],
            dst_ref=fresh.at[ch],
            send_sem=pair_send.at[ch],
            recv_sem=pair_recv.at[ch],
            device_id={"lat": other},
            device_id_type=mesh_ids,
        )

    def chip_copy(source, target, send_sems, recv_sems, ch, off):
        to = lax.rem(chip + off, chips)
        return pltpu.make_async_remote_copy(
            src_ref=source.at[ch, to],
            dst_ref=target.at[chip],
            send_sem=send_sems.at[ch, off - 1],
            recv_sem=recv_sems.at[ch, off - 1],
            device_id={"lat": to * 2 + core},
            device_id_type=mesh_ids,
        )

    def out_copy(ch, off):
        return chip_copy(send, land.at[ch], out_send, out_recv, ch, off)

    def in_copy(ch, off):
        return chip_copy(reply, home.at[ch, core], in_send, in_recv, ch, off)

    def hand_copy(ch, off):
        slot = lax.rem(chip + chips - off, chips)
        return pltpu.make_async_remote_copy(
            src_ref=home.at[ch, core, slot],
            dst_ref=home.at[ch, core, slot],
            send_sem=hand_send.at[ch, off],
            recv_sem=hand_recv.at[ch, off],
            device_id={"lat": other},
            device_id_type=mesh_ids,
        )

    def analyse(ch):
        for sub in range(subs):
            load(ch, sub).wait()

            def body(k, carry):
                x = sub * span + 2 * k
                pair = jnp.concatenate([u[ch % 2, x], u[ch % 2, x + 1]], axis=1)
                both = dot(basis[...], pair)
                high, low = halves(both[:modes] + both[modes:])
                for at in range(2):
                    highs[x + at] = high[:, at * CHUNK : (at + 1) * CHUNK]
                    lows[x + at] = low[:, at * CHUNK : (at + 1) * CHUNK]
                return carry

            lax.fori_loop(0, span // 2, body, 0, unroll=True)
        if ch + 2 < chunks:
            for sub in range(subs):
                load(ch + 2, sub).start()
        if ch == 0:
            for copy in tables():
                copy.wait()
        count = press.shape[0]
        for group in range(0, modes // 16, 2):
            stacks = []
            for g in (group, group + 1):
                take = slice(16 * g, 16 * g + 16)
                high = highs[:, take, :].reshape(rows * 16, CHUNK)
                low = lows[:, take, :].reshape(rows * 16, CHUNK)
                stacks.append(jnp.concatenate([high, low, high], axis=0))
            product = dot(press[...], jnp.concatenate(stacks, axis=1))
            half, within = divmod(group, modes // 32)
            for at in range(2):
                part[ch, half, count * (within + at) : count * (within + at + 1), :] = product[:, at * CHUNK : (at + 1) * CHUNK]

    def spill(value, target, ch):
        high = value.astype(jnp.bfloat16)
        cube = value.reshape(chips, tall, CHUNK)
        high_cube = high.reshape(chips, tall, CHUNK)
        low = cube[:, :lead] - high_cube[:, :lead].astype(jnp.float32)
        target[ch, :, :tall, :] = high_cube
        target[ch, :, tall:, :] = low.astype(jnp.bfloat16)

    def emit(ch):
        pair_copy(ch).wait_recv()
        spill(part[ch, core] + fresh[ch], send, ch)
        for off in range(1, chips):
            out_copy(ch, off).start()
        land[ch, chip] = send[ch, chip]

    def prepare():
        flat = modes_in[...]
        first = flat.astype(jnp.bfloat16)
        rest = flat - first.astype(jnp.float32)
        second = rest.astype(jnp.bfloat16)
        third = (rest - second.astype(jnp.float32)).astype(jnp.bfloat16)
        product = dot(jnp.concatenate([first, second, third], axis=0), picks[...])
        size = flat.shape[0]
        total = product[:size] + product[size : 2 * size] + product[2 * size :]
        for at in range(2 * chans - 1):
            diags[at] = total[:, at * 128 : (at + 1) * 128]
        half = folds.shape[1]
        local = exact(exact(spread_t[...], depth_local[...]), spread16[...]) * block_mask(half, chans, False)
        for side in range(2):
            mixer = exact(exact(sides[side], depth_in[...]), spread8[...]) * block_mask(folds.shape[2], chans, False)
            whole = 0.5 * exact(exact(folds[side], mixer), folds_t[side]) + 0.25 * local
            high, low = halves(whole)
            for at, x in enumerate((high, high, low)):
                depth_ops[side, at * half : (at + 1) * half, :] = x
        spot = exact(exact(spread_t[...], lat_local[...]), spread16[...]) * 0.5
        for side in range(2):
            high, low = halves(spot * block_mask(half, chans, side == 1))
            local_ops[side, :half, :] = high
            local_ops[side, half:, :] = low

    def ops_copies():
        return (
            pltpu.make_async_copy(depth_ops, depth_out, ops_sem.at[0]),
            pltpu.make_async_copy(local_ops, local_out, ops_sem.at[1]),
        )

    first_q = core * (modes // 2) + chip * held

    def blend(ch):
        for off in range(1, chips):
            out_copy(ch, off).wait_recv()
        high = land[ch, :, :tall, :].reshape(chips * tall, CHUNK)
        low = land[ch, :, tall:, :].reshape(chips * lead, CHUNK)
        coef = dot(front[...], jnp.concatenate([high, high, low], axis=0))
        scale = exact(gains[...], spread8[...])
        size = diags.shape[1]
        upper, lower = [], []
        for q in range(held):
            tile = coef[q * size : (q + 1) * size] * gains_row(scale, q)
            total = tile * diags[chans - 1]
            for at in range(2 * chans - 1):
                shift = at - (chans - 1)
                if shift != 0:
                    total += pltpu.roll(tile, (-shift) % 128, 1) * diags[at]
            if 2 * ch >= chunks:
                total = turn(total, chans)
            high, low = halves(total)
            upper.append(high)
            lower.append(low)
        spill(dot(back[...], jnp.concatenate(upper + lower + upper, axis=0)), reply, ch)
        for off in range(1, chips):
            in_copy(ch, off).start()
        home[ch, core, chip] = reply[ch, chip]
        hand_copy(ch, 0).start()

    def gains_row(scale, q):
        at = lax.broadcasted_iota(jnp.int32, scale.shape, 0)
        return jnp.sum(jnp.where(at == first_q + q, scale, 0.0), axis=0, keepdims=True)

    def hand(ch):
        for off in range(1, chips):
            in_copy(ch, off).wait_recv()
            hand_copy(ch, off).start()

    def place(ch):
        return ch if 2 * ch < chunks else chunks + chunks // 2 - 1 - ch

    def store_copies(ch):
        lanes = pl.ds(place(ch) * CHUNK, CHUNK)
        return (
            pltpu.make_async_copy(wide_high.at[ch], high_out.at[:, :, lanes], store_sem.at[ch, 0]),
            pltpu.make_async_copy(wide_low.at[ch], low_out.at[:, :, lanes], store_sem.at[ch, 1]),
        )

    def expand(ch):
        for off in range(chips):
            hand_copy(ch, off).wait_recv()
        each = 16 // held
        for group in range(0, modes // 16, 2):
            stacks = []
            for g in (group, group + 1):
                half, within = divmod(g, modes // 32)
                take = slice(each * within, each * (within + 1))
                high = home[ch, half, take, :tall, :].reshape(each * tall, CHUNK)
                low = home[ch, half, take, tall:, :].reshape(each * lead, CHUNK)
                stacks.append(jnp.concatenate([high, high, low], axis=0))
            high, low = halves(dot(grow[...], jnp.concatenate(stacks, axis=1)))
            for at in range(2):
                take = slice(16 * (group + at), 16 * (group + at + 1))
                lanes = slice(at * CHUNK, (at + 1) * CHUNK)
                wide_high[ch, :, take, :] = high[:, lanes].reshape(rows, 16, CHUNK)
                wide_low[ch, :, take, :] = low[:, lanes].reshape(rows, 16, CHUNK)
        for copy in store_copies(ch):
            copy.start()

    analyse(0)
    pl.semaphore_wait(barrier, chips)
    pair_copy(0).start()
    for ch in range(1, chunks):
        analyse(ch)
        pair_copy(ch).start()
        emit(ch - 1)
    emit(chunks - 1)
    prepare()
    for copy in ops_copies():
        copy.start()
    for ch in range(chunks):
        blend(ch)
        if ch >= 1:
            hand(ch - 1)
        if ch >= 2:
            expand(ch - 2)
    hand(chunks - 1)
    expand(chunks - 2)
    expand(chunks - 1)
    for ch in range(chunks):
        pair_copy(ch).wait_send()
        for off in range(1, chips):
            out_copy(ch, off).wait_send()
            in_copy(ch, off).wait_send()
        for off in range(chips):
            hand_copy(ch, off).wait_send()
        for copy in store_copies(ch):
            copy.wait()
    for copy in ops_copies():
        copy.wait()


def exchange(chips, held, rank, chans, *args):
    field, press_all, grow_all, basis = args[:4]
    rows, width, cells = field.shape
    modes = basis.shape[0] // 2
    chunks = cells // CHUNK
    tall, lead = held * rank, held * LEAD
    half = cells // 2
    size = args[7].shape[0]
    hbm = pl.BlockSpec(memory_space=pl.ANY)
    whole = lambda a: pl.BlockSpec(a.shape, lambda: (0,) * a.ndim)
    dma = pltpu.SemaphoreType.DMA
    bf16, f32 = jnp.bfloat16, jnp.float32
    blocks = (chunks, chips, tall + lead, CHUNK)
    return pl.pallas_call(
        functools.partial(exchange_kernel, chips, held, rank, chans),
        in_specs=[hbm] * 3 + [whole(a) for a in args[3:]],
        out_specs=[hbm] * 4,
        out_shape=[
            jax.ShapeDtypeStruct((rows, modes, cells), bf16),
            jax.ShapeDtypeStruct((rows, modes, cells), bf16),
            jax.ShapeDtypeStruct((2, 3 * half, half), bf16),
            jax.ShapeDtypeStruct((2, 2 * half, half), bf16),
        ],
        scratch_shapes=[
            pltpu.VMEM((2, rows, width, CHUNK), bf16),
            pltpu.VMEM(press_all.shape[1:], bf16),
            pltpu.VMEM(grow_all.shape[1:], bf16),
            pltpu.VMEM((rows, modes, CHUNK), bf16),
            pltpu.VMEM((rows, modes, CHUNK), bf16),
            pltpu.VMEM((chunks, 2, chips * tall, CHUNK), f32),
            pltpu.VMEM((chunks, chips * tall, CHUNK), f32),
            pltpu.VMEM(blocks, bf16),
            pltpu.VMEM(blocks, bf16),
            pltpu.VMEM(blocks, bf16),
            pltpu.VMEM((chunks, 2) + blocks[1:], bf16),
            pltpu.VMEM((chunks, rows, modes, CHUNK), bf16),
            pltpu.VMEM((chunks, rows, modes, CHUNK), bf16),
            pltpu.VMEM((2 * chans - 1, size, 128), f32),
            pltpu.VMEM((2, 3 * half, half), bf16),
            pltpu.VMEM((2, 2 * half, half), bf16),
            dma((chunks, 4)),
            dma((2,)),
            dma((chunks,)),
            dma((chunks,)),
            dma((chunks, chips - 1)),
            dma((chunks, chips - 1)),
            dma((chunks, chips - 1)),
            dma((chunks, chips - 1)),
            dma((chunks, chips)),
            dma((chunks, chips)),
            dma((chunks, 2)),
            dma((2,)),
        ],
        compiler_params=pltpu.CompilerParams(collective_id=5, has_side_effects=True, vmem_limit_bytes=58 * MIB),
    )(*args)


def finish_kernel(chans, u_ref, high_ref, low_ref, basis_ref, local_ref, depth_ref, out_ref, *rhs):
    rows, width, cells = u_ref.shape
    half = cells // 2
    modes = high_ref.shape[1]

    @pl.when(pl.program_id(0) == 0)
    def _():
        for r in rhs:
            r[:, 4 * modes :, :] = local_ref[...]

    def first_layer(row):
        high, low = high_ref[row], low_ref[row]
        parts = []
        for side in range(2):
            lanes = slice(side * half, (side + 1) * half)
            for k, x in enumerate((high, low, high, low)):
                rhs[row][side, modes * k : modes * (k + 1), :] = x[:, lanes]
            u = u_ref[row, :, lanes]
            h = dot(jnp.concatenate([basis_ref[...], u, u], axis=1), rhs[row][side])
            wide = u.astype(jnp.float32)
            parts.append((turn(wide, chans) if side else wide) + act(h))
        return parts

    def second_layer(row, first):
        mixes = []
        for side, x in enumerate((first[0] + first[1], first[0] - first[1])):
            high, low = halves(x)
            mixes.append(dot(jnp.concatenate([high, low, high], axis=1), depth_ref[side]))
        upper = first[1] + act(mixes[0] - mixes[1])
        out_ref[row, :, :half] = (first[0] + act(mixes[0] + mixes[1])).astype(out_ref.dtype)
        out_ref[row, :, half:] = turn(upper, chans).astype(out_ref.dtype)

    firsts = [first_layer(0)]
    for row in range(rows):
        if row + 1 < rows:
            firsts.append(first_layer(row + 1))
        second_layer(row, firsts[row])


def finish(field, high, low, basis, local, depth, chans):
    rows, width, cells = field.shape
    modes = high.shape[1]
    step = math.gcd(rows, 2)
    whole = lambda a: pl.BlockSpec(a.shape, lambda i: (0,) * a.ndim)
    block = pl.BlockSpec((step, width, cells), lambda i: (i, 0, 0))
    thin = pl.BlockSpec((step, modes, cells), lambda i: (i, 0, 0))
    return pl.pallas_call(
        functools.partial(finish_kernel, chans),
        grid=(rows // step,),
        in_specs=[block, thin, thin, whole(basis), whole(local), whole(depth)],
        out_specs=block,
        out_shape=jax.ShapeDtypeStruct(field.shape, jnp.bfloat16),
        scratch_shapes=[pltpu.VMEM((2, 4 * modes + cells, cells // 2), jnp.bfloat16)] * step,
        compiler_params=pltpu.CompilerParams(vmem_limit_bytes=56 * MIB),
        cost_estimate=pl.CostEstimate(
            flops=2 * rows * width * cells * (3 * cells),
            bytes_accessed=4 * rows * width * cells,
            transcendentals=2 * rows * width * cells,
        ),
    )(field, high, low, basis, local, depth)


def stack_halves(x, order, axis):
    pair = np_halves(np.asarray(x, dtype=np.float32))
    return np.concatenate([pair[k] for k in order], axis=axis)


def shards_chips(devices, factors, field, lat_modes, lat_gains, lat_local, depth_modes, depth_local):
    rows, width_y, cells = field.shape
    modes_x, chans, _ = lat_modes.shape
    modes_y = lat_gains.shape[0]
    modes_z = depth_modes.shape[0]
    depth = cells // chans
    chips = devices // 2
    held = modes_y // devices
    basis_y = cosine_basis(width_y, modes_y)
    basis_z = cosine_basis(depth, modes_z)
    left, right = factors
    rank = left.shape[2]
    tall, lead, each = held * rank, held * LEAD, 16 // held

    order = [(q, j) for q in range(held) for j in range(LEAD)]
    order += [(q, j) for q in range(held) for j in range(LEAD, rank)]
    slots = np.array([q * rank + j for q, j in order])

    own = right.reshape(chips, rank, 2, rows).transpose(0, 2, 1, 3).reshape(devices, rank, rows)
    kron = np.einsum("djx,qr->dqjxr", own, np.eye(16)).reshape(devices, each, tall, rows * 16)
    kron = kron[:, :, slots].reshape(devices, each * tall, rows * 16)
    press = stack_halves(kron, (0, 0, 1), 2)
    grown = np.float32(0.5 * kron.transpose(0, 2, 1))
    high, low = np_halves(grown)
    leads = high.reshape(devices, rows * 16, each, tall)[..., :lead].reshape(devices, rows * 16, each * lead)
    grow = np.concatenate([high, low, leads], axis=2)

    sides = np.einsum("ipj,qr->qpirj", left, np.eye(held)).reshape(held * modes_x, chips, tall)
    sides = sides[:, :, slots]
    flat = np.float32(sides.reshape(held * modes_x, chips * tall))
    high, low = np_halves(flat)
    leads = high.reshape(held * modes_x, chips, tall)[..., :lead].reshape(held * modes_x, chips * lead)
    front = np.concatenate([high, low, leads], axis=1)
    back = stack_halves(flat.T, (0, 0, 1), 1)
    front_y = stack_halves(basis_y, (0, 1), 0)
    back_y = stack_halves(basis_y.T, (0, 0, 1, 1), 1)

    places = np.arange(chans)
    shift = np.arange(2 * chans - 1) - (chans - 1)
    pick = (places[:, None, None, None] == (places[None, None, None, :] + shift[None, None, :, None])) & (
        places[None, :, None, None] == places[None, None, None, :]
    )
    picks = np.tile(pick.reshape(chans * chans, 2 * chans - 1, chans), (1, 1, 128 // chans))
    picks = picks.reshape(chans * chans, -1).astype(jnp.bfloat16)

    half = depth // 2
    folds = np.stack([np.kron(basis_z[side::2, :half].T, np.eye(chans)) for side in range(2)]).astype(np.float32)
    kinds = np.eye(modes_z)
    sides_z = np.stack([np.kron(kinds[side::2], np.eye(chans)) for side in range(2)]).astype(np.float32)
    spread8 = np.tile(np.eye(chans, dtype=np.float32), (1, modes_z // 2))
    spread16 = np.tile(np.eye(chans, dtype=np.float32), (1, half))

    consts = [jnp.asarray(a) for a in (press, grow, front_y, front, back)]
    more = [jnp.asarray(a) for a in (picks, folds, folds.transpose(0, 2, 1).copy(), sides_z, spread8, spread16, spread16.T.copy())]
    args = [field] + consts + [lat_gains, lat_modes.reshape(modes_x, chans * chans)] + more
    args += [depth_modes.reshape(modes_z * chans, chans), depth_local, lat_local]
    high, low, depth_ops, local_ops = exchange(chips, held, rank, chans, *args)
    return finish(field, high, low, jnp.asarray(back_y), local_ops, depth_ops, chans)


def wide_basis(length, modes):
    order = np.arange(modes, dtype=np.float64)[:, None]
    place = np.arange(length, dtype=np.float64)[None, :]
    scales = np.where(order == 0.0, math.sqrt(1.0 / length), math.sqrt(2.0 / length))
    return np.cos(math.pi * order * (place + 0.5) / length) * scales


def shards(field, lat_modes, lat_gains, lat_local, depth_modes, depth_local):
    devices = lax.axis_size("lat")
    rows, _, cells = field.shape
    modes_x, chans, _ = lat_modes.shape
    modes_y, modes_z = lat_gains.shape[0], depth_modes.shape[0]
    args = (field, lat_modes, lat_gains, lat_local, depth_modes, depth_local)
    fits = devices % 2 == 0 and modes_y % (2 * devices) == 0 and modes_y % 64 == 0 and 16 % (modes_y // devices) == 0
    fits = fits and rows % 8 == 0 and cells % (4 * CHUNK) == 0 and chans * modes_z == 256 and cells == 512 and chans * chans == 256
    if fits:
        held = modes_y // devices
        factors = window_factors(wide_basis(rows * devices, modes_x), devices // 2, max(1, 16 // held))
        if factors[0].shape[2] >= LEAD and held * LEAD % 16 == 0:
            return shards_chips(devices, factors, *args)
    return shards_rows(*args)


def solution(mesh):
    placed = (P(("group", "lat"), None, None), P(), P(), P(), P(), P())
    return jax.shard_map(
        shards,
        mesh=mesh,
        in_specs=placed,
        out_specs=P(("group", "lat"), None, None),
        check_vma=False,
    )
```

```python
import functools
import math

import jax
import jax.numpy as jnp
import numpy as np
from jax import lax
from jax.experimental import pallas as pl
from jax.experimental.pallas import tpu as pltpu
from jax.sharding import PartitionSpec as P

LINK = jnp.float16
SCALE_OUT = 256.0
SCALE_BACK = 1.0 / 16.0
K0 = math.sqrt(2.0 / math.pi)
K1 = K0 * 0.044715
MIB = 1 << 20


def cosine_basis(length, modes):
    order = np.arange(modes, dtype=np.float64)[:, None]
    place = np.arange(length, dtype=np.float64)[None, :]
    scales = np.where(order == 0.0, math.sqrt(1.0 / length), math.sqrt(2.0 / length))
    return (np.cos(math.pi * order * (place + 0.5) / length) * scales).astype(np.float32)


def halves(x):
    high = jnp.asarray(x).astype(jnp.bfloat16)
    low = (x - high.astype(jnp.float32)).astype(jnp.bfloat16)
    return high, low


def outer_halves(x):
    high = lax.reduce_precision(x, 8, 7)
    return high.astype(jnp.bfloat16), (x - high).astype(jnp.bfloat16)


def np_halves(x):
    high = np.asarray(x, dtype=jnp.bfloat16)
    low = np.asarray(x - high.astype(np.float32), dtype=jnp.bfloat16)
    return high, low


def dot(a, b):
    return jnp.dot(a, b, preferred_element_type=jnp.float32)


def gelu(x):
    half = 0.5 * x
    return half + half * jnp.tanh(x * (K0 + K1 * (x * x)))


def forward_kernel(basis_ref, u_ref, out_ref):
    modes = out_ref.shape[1]

    def body(row, carry):
        both = dot(basis_ref[...], u_ref[row])
        out_ref[row] = (both[:modes] + both[modes:]) * SCALE_OUT
        return carry

    lax.fori_loop(0, u_ref.shape[0], body, 0)


def forward(field, basis, start, rows):
    _, width, cells = field.shape
    modes = basis.shape[0] // 2
    step = math.gcd(rows, 4)
    return pl.pallas_call(
        forward_kernel,
        grid=(rows // step,),
        in_specs=[
            pl.BlockSpec(basis.shape, lambda i: (0, 0)),
            pl.BlockSpec((step, width, cells), lambda i: (i + start // step, 0, 0)),
        ],
        out_specs=pl.BlockSpec((step, modes, cells), lambda i: (i, 0, 0)),
        out_shape=jax.ShapeDtypeStruct((rows, modes, cells), jnp.float32),
        compiler_params=pltpu.CompilerParams(vmem_limit_bytes=40 * MIB),
        cost_estimate=pl.CostEstimate(
            flops=4 * rows * modes * width * cells,
            bytes_accessed=rows * cells * (2 * width + 4 * modes),
            transcendentals=0,
        ),
    )(basis, field)


def middle_kernel(chunks, chans, *refs):
    g_refs = refs[:chunks]
    f_refs = refs[chunks : 2 * chunks]
    b_refs = refs[2 * chunks : 3 * chunks]
    gain_ref, diag_ref = refs[3 * chunks : 3 * chunks + 2]
    out_refs = refs[3 * chunks + 2 :]
    modes = diag_ref.shape[1]
    coef = None
    for g_ref, f_ref in zip(g_refs, f_refs):
        high, low = halves(g_ref[0])
        both = dot(f_ref[...], high)
        part = both[:modes] + both[modes:] + dot(f_ref[:modes], low)
        coef = part if coef is None else coef + part
    coef = coef * gain_ref[0]
    tiles = []
    for lane in range(0, coef.shape[1], 128):
        tile = coef[:, lane : lane + 128]
        total = tile * diag_ref[chans - 1]
        for at in range(2 * chans - 1):
            shift = at - (chans - 1)
            if shift != 0:
                total += pltpu.roll(tile, (-shift) % 128, 1) * diag_ref[at]
        tiles.append(total)
    mixed = jnp.concatenate(tiles, axis=1) if len(tiles) > 1 else tiles[0]
    high, low = halves(mixed)
    stacked = jnp.concatenate([high, low, high], axis=0)
    for b_ref, out_ref in zip(b_refs, out_refs):
        out_ref[0] = dot(b_ref[...], stacked)


def middle(gathered, fronts, backs, gains, diags):
    chunks = len(gathered)
    count, length, width = gathered[0].shape
    modes = diags.shape[1]
    chans = (diags.shape[0] + 1) // 2
    whole = lambda a: pl.BlockSpec(a.shape, lambda i: (0,) * a.ndim)
    block = pl.BlockSpec((1, length, width), lambda i: (i, 0, 0))
    return pl.pallas_call(
        functools.partial(middle_kernel, chunks, chans),
        grid=(count,),
        in_specs=[block] * chunks
        + [whole(a) for a in fronts]
        + [whole(a) for a in backs]
        + [pl.BlockSpec((1, 1, width), lambda i: (i, 0, 0)), whole(diags)],
        out_specs=[block] * chunks,
        out_shape=[jax.ShapeDtypeStruct((count, length, width), jnp.float32)] * chunks,
        compiler_params=pltpu.CompilerParams(vmem_limit_bytes=40 * MIB),
    )(*gathered, *fronts, *backs, gains, diags)


def tail_kernel(piece, u_ref, back_ref, basis_ref, local_ref, depth_ref, *refs):
    out_ref = refs[-1]
    _, width, cells = u_ref.shape
    block = local_ref.shape[1]
    high, low = halves(back_ref[0])
    stacked = jnp.concatenate([high, low, high], axis=0)

    def body(at, carry):
        rows = pl.ds(pl.multiple_of(at * piece, piece), piece)
        u = u_ref[0, rows, :]
        spect = dot(basis_ref[rows, :], stacked)
        parts = []
        for lane in range(0, cells, block):
            tile = u[:, lane : lane + block]
            parts.append(dot(tile, local_ref[0]) + dot(tile, local_ref[1]))
        local = jnp.concatenate(parts, axis=1) if len(parts) > 1 else parts[0]
        first = u.astype(jnp.float32) + gelu(spect + local)
        high1, low1 = halves(first)
        mix = dot(high1, depth_ref[0]) + dot(low1, depth_ref[0]) + dot(high1, depth_ref[1])
        out_ref[0, rows, :] = (first + gelu(mix)).astype(out_ref.dtype)
        return carry

    lax.fori_loop(0, width // piece, body, 0)


def tail(field, back, basis, local, depth, previous, start):
    rows, modes, cells = back.shape
    width = field.shape[1]
    whole = lambda a: pl.BlockSpec(a.shape, lambda i: (0,) * a.ndim)
    operands = [field, back, basis, local, depth]
    specs = [
        pl.BlockSpec((1, width, cells), lambda i: (i + start, 0, 0)),
        pl.BlockSpec((1, modes, cells), lambda i: (i, 0, 0)),
        whole(basis),
        whole(local),
        whole(depth),
    ]
    aliases = {}
    if previous is not None:
        aliases = {len(operands): 0}
        operands.append(previous)
        specs.append(pl.BlockSpec(memory_space=pl.ANY))
    return pl.pallas_call(
        functools.partial(tail_kernel, math.gcd(width, 256)),
        grid=(rows,),
        in_specs=specs,
        out_specs=pl.BlockSpec((1, width, cells), lambda i: (i + start, 0, 0)),
        out_shape=jax.ShapeDtypeStruct(field.shape, jnp.bfloat16),
        input_output_aliases=aliases,
        compiler_params=pltpu.CompilerParams(vmem_limit_bytes=48 * MIB),
        cost_estimate=pl.CostEstimate(
            flops=2 * rows * width * cells * (4 * cells),
            bytes_accessed=4 * rows * width * cells,
            transcendentals=2 * rows * width * cells,
        ),
    )(*operands)


def block_diagonal(small, size):
    chans = small.shape[0]
    copies = size // chans
    ids = np.arange(size) // chans
    mask = (ids[:, None] == ids[None, :]).astype(np.float32)
    return jnp.tile(small, (copies, copies)) * mask


def shards_rows(field, lat_modes, lat_gains, lat_local, depth_modes, depth_local):
    highest = lax.Precision.HIGHEST
    devices = lax.axis_size("lat")
    rows_dev, width_y, cells = field.shape
    modes_x, chans, _ = lat_modes.shape
    modes_y = lat_gains.shape[0]
    modes_z = depth_modes.shape[0]
    depth = cells // chans
    width_x = rows_dev * devices
    chunks = 2 if rows_dev % 16 == 0 else 1
    rows = rows_dev // chunks
    splits = max(1, devices // modes_y)
    held = modes_y * splits // devices
    span = cells // splits
    basis_x = cosine_basis(width_x, modes_x)
    basis_y = cosine_basis(width_y, modes_y)
    basis_z = cosine_basis(depth, modes_z)

    high_y, low_y = np_halves(basis_y)
    front_y = jnp.asarray(np.concatenate([high_y, low_y], axis=0))
    back_y = jnp.asarray(np.concatenate([high_y, high_y, low_y], axis=0).T.copy())
    fronts, backs = [], []
    for chunk in range(chunks):
        part = basis_x.reshape(modes_x, devices, chunks, rows)[:, :, chunk].reshape(modes_x, -1)
        high_x, low_x = np_halves(part)
        fronts.append(jnp.asarray(np.concatenate([high_x, low_x], axis=0)))
        backs.append(jnp.asarray(np.concatenate([high_x, high_x, low_x], axis=0).T.copy()))

    gathered = []
    for chunk in range(chunks):
        coef_y = forward(field, front_y, chunk * rows, rows)
        sent = coef_y.astype(LINK).reshape(rows, modes_y, splits, span)
        sent = sent.transpose(1, 2, 0, 3).reshape(modes_y * splits, rows, span)
        gathered.append(lax.all_to_all(sent, "lat", split_axis=0, concat_axis=0, tiled=True))

    shift = np.arange(2 * chans - 1)[:, None, None] - (chans - 1)
    places = np.arange(chans)
    pick = (places[None, :, None] == places[None, None, :] + shift).astype(np.float32)
    diags = jnp.sum(lat_modes[None] * pick[:, None], axis=2)
    diags = jnp.tile(diags, (1, 1, 128 // chans))
    me = lax.axis_index("lat")
    gain_rows = lax.dynamic_slice_in_dim(lat_gains, me * held // splits, held, 0)
    gain_rows = jnp.tile(gain_rows * (SCALE_BACK / SCALE_OUT), (1, span // chans))[:, None, :]

    spread = np.kron(basis_z.T, np.eye(chans, dtype=np.float32))
    ids = np.arange(modes_z * chans) // chans
    mask = (ids[:, None] == ids[None, :]).astype(np.float32)
    mixers = jnp.tile(depth_modes.reshape(modes_z * chans, chans), (1, modes_z)) * mask
    inner = jnp.dot(mixers, spread.T, precision=highest)
    whole = jnp.dot(spread, inner, precision=highest) + block_diagonal(depth_local, cells)
    depth_pair = jnp.stack(outer_halves(whole))
    local_pair = jnp.stack(outer_halves(block_diagonal(lat_local, math.gcd(cells, 256))))

    received = []
    for got in gathered:
        got = got.reshape(devices, held, rows, span).transpose(1, 0, 2, 3).astype(jnp.float32)
        received.append(got.reshape(held, devices * rows, span))
    mixed = middle(received, fronts, backs, gain_rows, diags)
    returned = []
    for part in mixed:
        part = part.astype(LINK).reshape(held, devices, rows, span).transpose(1, 0, 2, 3)
        part = part.reshape(devices * held, rows, span)
        returned.append(lax.all_to_all(part, "lat", split_axis=0, concat_axis=0, tiled=True))
    out = None
    for chunk, part in enumerate(returned):
        part = part.reshape(modes_y, splits, rows, span).transpose(2, 0, 1, 3)
        part = part.reshape(rows, modes_y, cells).astype(jnp.float32) * (1.0 / SCALE_BACK)
        out = tail(field, part, back_y, local_pair, depth_pair, out, chunk * rows)
    return out

LINK_OUT = 64.0
LINK_BACK = 1.0 / 32.0
C0 = 2.0 * K0
C1 = 8.0 * K1


def act(h):
    return h + h * jnp.tanh(h * (C0 + C1 * (h * h)))


def window_factors(basis, windows, fine):
    modes = basis.shape[0]
    blocks = basis.reshape(modes, windows, -1).transpose(1, 0, 2)
    left, sizes, right = np.linalg.svd(blocks, full_matrices=False)
    left = left * sizes[:, None, :]
    top = np.abs(basis).max()
    rank = fine
    while rank < sizes.shape[1]:
        product = left[:, :, :rank] @ right[:, :rank]
        if np.abs(product - blocks).max() <= 2.0 ** -23 * top:
            break
        rank += fine
    return left[:, :, :rank], right[:, :rank]


def turn(x, unit):
    place = lax.broadcasted_iota(jnp.int32, (x.shape[0], 128), 1)
    place = (128 - unit - place // unit * unit) + place % unit
    tiles = [jnp.take_along_axis(x[:, at : at + 128], place, axis=1) for at in range(0, x.shape[1], 128)]
    return jnp.concatenate(tiles[::-1], axis=1)


LEAD = 9
CHUNK = 128


def exact(a, b):
    return jnp.dot(a, b, preferred_element_type=jnp.float32, precision=lax.Precision.HIGHEST)


def turned_dot(a, b, precision=None):
    return lax.dot_general(a, b, (((0,), (0,)), ((), ())), precision=precision, preferred_element_type=jnp.float32)


def block_mask(size, unit, flip):
    row = lax.broadcasted_iota(jnp.int32, (size, size), 0) // unit
    lane = lax.broadcasted_iota(jnp.int32, (size, size), 1) // unit
    return (row == (size // unit - 1 - lane if flip else lane)).astype(jnp.float32)


def exchange_kernel(chips, held, tall, chans, *refs):
    field, press_all, grow_all, front_in, back_in, picks_in, folds_in, folds_t_in, sides_in = refs[:9]
    (basis, gains, modes_in, spread8, spread16, spread_t, depth_in, depth_local, lat_local, high_out, low_out, depth_out, local_out) = refs[9:22]
    (u, highs, lows, part, fresh, send, land, reply, home, wide_high, wide_low, diags, depth_ops, local_ops) = refs[22:36]
    press, grow, front, back, picks, folds, folds_t, sides = refs[36:44]
    load_sem, table_sem, pair_send, pair_recv, out_send, out_recv, in_send, in_recv, hand_send, hand_recv, store_sem, ops_sem = refs[44:]
    rows, width, cells = field.shape
    modes = basis.shape[0] // 2
    chunks = cells // CHUNK
    block = send.shape[2]
    mesh_ids = pl.DeviceIdType.MESH
    me = lax.axis_index("lat")
    chip, core = me // 2, lax.rem(me, 2)
    other = chip * 2 + 1 - core
    subs = 4
    span = rows // subs

    def load(ch, sub):
        take = pl.ds(sub * span, span)
        return pltpu.make_async_copy(
            field.at[take, :, pl.ds(ch * CHUNK, CHUNK)], u.at[ch % 2, take], load_sem.at[ch, sub]
        )

    def tables():
        sources = (press_all.at[me], grow_all.at[me], front_in, back_in, picks_in, folds_in, folds_t_in, sides_in)
        targets = (press, grow, front, back, picks, folds, folds_t, sides)
        pairs = enumerate(zip(sources, targets))
        return [pltpu.make_async_copy(source, target, table_sem.at[k]) for k, (source, target) in pairs]

    for sub in range(subs):
        load(0, sub).start()
    tables()[0].start()
    for sub in range(subs):
        load(1, sub).start()
    for copy in tables()[1:]:
        copy.start()

    barrier = pltpu.get_barrier_semaphore()
    for off in range(1, chips):
        peer = lax.rem(chip + off, chips) * 2 + core
        pl.semaphore_signal(barrier, inc=1, device_id={"lat": peer}, device_id_type=mesh_ids)
    pl.semaphore_signal(barrier, inc=1, device_id={"lat": other}, device_id_type=mesh_ids)

    def pair_copy(ch):
        return pltpu.make_async_remote_copy(
            src_ref=part.at[ch, 1 - core],
            dst_ref=fresh.at[ch],
            send_sem=pair_send.at[ch],
            recv_sem=pair_recv.at[ch],
            device_id={"lat": other},
            device_id_type=mesh_ids,
        )

    def chip_copy(source, target, send_sems, recv_sems, ch, off):
        to = lax.rem(chip + off, chips)
        return pltpu.make_async_remote_copy(
            src_ref=source.at[ch, to],
            dst_ref=target.at[chip],
            send_sem=send_sems.at[ch, off - 1],
            recv_sem=recv_sems.at[ch, off - 1],
            device_id={"lat": to * 2 + core},
            device_id_type=mesh_ids,
        )

    def out_copy(ch, off):
        return chip_copy(send, land.at[ch], out_send, out_recv, ch, off)

    def in_copy(ch, off):
        return chip_copy(reply, home.at[ch, core], in_send, in_recv, ch, off)

    def hand_copy(ch, off):
        slot = lax.rem(chip + chips - off, chips)
        return pltpu.make_async_remote_copy(
            src_ref=home.at[ch, core, slot],
            dst_ref=home.at[ch, core, slot],
            send_sem=hand_send.at[ch, off],
            recv_sem=hand_recv.at[ch, off],
            device_id={"lat": other},
            device_id_type=mesh_ids,
        )

    def analyse(ch):
        for sub in range(subs):
            load(ch, sub).wait()

            def body(k, carry):
                x = sub * span + 2 * k
                pair = jnp.concatenate([u[ch % 2, x], u[ch % 2, x + 1]], axis=1)
                both = dot(basis[...], pair)
                high, low = halves(both[:modes] + both[modes:])
                for at in range(2):
                    highs[x + at] = high[:, at * CHUNK : (at + 1) * CHUNK]
                    lows[x + at] = low[:, at * CHUNK : (at + 1) * CHUNK]
                return carry

            lax.fori_loop(0, span // 2, body, 0, unroll=True)
        if ch + 2 < chunks:
            for sub in range(subs):
                load(ch + 2, sub).start()
        if ch == 0:
            tables()[0].wait()
        count = press.shape[0]
        for group in range(0, modes // 16, 2):
            stacks = []
            for g in (group, group + 1):
                take = slice(16 * g, 16 * g + 16)
                high = highs[:, take, :].reshape(rows * 16, CHUNK)
                low = lows[:, take, :].reshape(rows * 16, CHUNK)
                stacks.append(jnp.concatenate([high, low, high], axis=0))
            product = dot(press[...], jnp.concatenate(stacks, axis=1))
            half, within = divmod(group, modes // 32)
            for at in range(2):
                part[ch, half, count * (within + at) : count * (within + at + 1), :] = product[:, at * CHUNK : (at + 1) * CHUNK]

    def spill(value, target, ch):
        high, low = halves(value)
        place = lax.broadcasted_iota(jnp.int32, value.shape, 0) % block
        target[ch] = jnp.where(place < tall, high, low).reshape(chips, block, CHUNK)

    def emit(ch):
        pair_copy(ch).wait_recv()
        spill(part[ch, core] + fresh[ch], send, ch)
        for off in range(1, chips):
            out_copy(ch, off).start()
        land[ch, chip] = send[ch, chip]

    def prepare():
        rest, total = modes_in[...], None
        for _ in range(3):
            term = rest.astype(jnp.bfloat16)
            rest = rest - term.astype(jnp.float32)
            product = turned_dot(term, picks[...])
            total = product if total is None else total + product
        for at in range(2 * chans - 1):
            diags[at] = total[:, at * 128 : (at + 1) * 128]
        half = folds.shape[1]
        local = exact(exact(spread_t[...], depth_local[...]), spread16[...]) * block_mask(half, chans, False)
        for side in range(2):
            mixer = exact(exact(sides[side], depth_in[...]), spread8[...]) * block_mask(folds.shape[2], chans, False)
            whole = 0.5 * exact(exact(folds[side], mixer), folds_t[side]) + 0.25 * local
            high, low = halves(whole)
            for at, x in enumerate((high, high, low)):
                depth_ops[side, at * half : (at + 1) * half, :] = x
        spot = exact(exact(spread_t[...], lat_local[...]), spread16[...]) * 0.5
        for side in range(2):
            high, low = halves(spot * block_mask(half, chans, side == 1))
            local_ops[side, :half, :] = high
            local_ops[side, half:, :] = low

    def ops_copies():
        return (
            pltpu.make_async_copy(depth_ops, depth_out, ops_sem.at[0]),
            pltpu.make_async_copy(local_ops, local_out, ops_sem.at[1]),
        )

    first_q = core * (modes // 2) + chip * held

    def blend(ch):
        for off in range(1, chips):
            out_copy(ch, off).wait_recv()
        values = land[ch].reshape(chips * block, CHUNK)
        coef = dot(front[...], jnp.concatenate([values, values], axis=0))
        scale = turned_dot(gains[...], spread8[...], lax.Precision.HIGHEST)
        size = diags.shape[1]
        upper, lower = [], []
        for q in range(held):
            tile = coef[q * size : (q + 1) * size] * gains_row(scale, q)
            total = tile * diags[chans - 1]
            for at in range(2 * chans - 1):
                shift = at - (chans - 1)
                if shift != 0:
                    total += pltpu.roll(tile, (-shift) % 128, 1) * diags[at]
            if 2 * ch >= chunks:
                total = turn(total, chans)
            high, low = halves(total)
            upper.append(high)
            lower.append(low)
        spill(dot(back[...], jnp.concatenate(upper + lower + upper, axis=0)), reply, ch)
        for off in range(1, chips):
            in_copy(ch, off).start()
        home[ch, core, chip] = reply[ch, chip]
        hand_copy(ch, 0).start()

    def gains_row(scale, q):
        at = lax.broadcasted_iota(jnp.int32, scale.shape, 0)
        return jnp.sum(jnp.where(at == first_q + q, scale, 0.0), axis=0, keepdims=True)

    def hand(ch):
        for off in range(1, chips):
            in_copy(ch, off).wait_recv()
            hand_copy(ch, off).start()

    def place(ch):
        return ch if 2 * ch < chunks else chunks + chunks // 2 - 1 - ch

    def store_copies(ch):
        lanes = pl.ds(place(ch) * CHUNK, CHUNK)
        return (
            pltpu.make_async_copy(wide_high.at[ch], high_out.at[:, :, lanes], store_sem.at[ch, 0]),
            pltpu.make_async_copy(wide_low.at[ch], low_out.at[:, :, lanes], store_sem.at[ch, 1]),
        )

    def expand(ch):
        for off in range(chips):
            hand_copy(ch, off).wait_recv()
        each = 16 // held
        for group in range(0, modes // 16, 2):
            stacks = []
            for g in (group, group + 1):
                half, within = divmod(g, modes // 32)
                take = slice(each * within, each * (within + 1))
                values = home[ch, half, take].reshape(each * block, CHUNK)
                stacks.append(jnp.concatenate([values, values], axis=0))
            high, low = halves(dot(grow[...], jnp.concatenate(stacks, axis=1)))
            for at in range(2):
                take = slice(16 * (group + at), 16 * (group + at + 1))
                lanes = slice(at * CHUNK, (at + 1) * CHUNK)
                wide_high[ch, :, take, :] = high[:, lanes].reshape(rows, 16, CHUNK)
                wide_low[ch, :, take, :] = low[:, lanes].reshape(rows, 16, CHUNK)
        for copy in store_copies(ch):
            copy.start()

    analyse(0)
    pl.semaphore_wait(barrier, chips)
    pair_copy(0).start()
    emit(0)
    for ch in range(1, chunks):
        analyse(ch)
        pair_copy(ch).start()
        if ch > 1:
            emit(ch - 1)
    emit(chunks - 1)
    for copy in tables()[1:]:
        copy.wait()
    prepare()
    for copy in ops_copies():
        copy.start()
    for ch in range(chunks):
        blend(ch)
    for ch in range(chunks):
        hand(ch)
        if ch >= 1:
            expand(ch - 1)
    expand(chunks - 1)
    for ch in range(chunks):
        pair_copy(ch).wait_send()
        for off in range(1, chips):
            out_copy(ch, off).wait_send()
            in_copy(ch, off).wait_send()
        for off in range(chips):
            hand_copy(ch, off).wait_send()
        for copy in store_copies(ch):
            copy.wait()
    for copy in ops_copies():
        copy.wait()


def exchange(chips, held, tall, block, chans, *args):
    field, press_all, grow_all = args[:3]
    basis, gains = args[9:11]
    rows, width, cells = field.shape
    modes = basis.shape[0] // 2
    chunks = cells // CHUNK
    half = cells // 2
    size = args[11].shape[1]
    hbm = pl.BlockSpec(memory_space=pl.ANY)
    whole = lambda a: pl.BlockSpec(a.shape, lambda: (0,) * a.ndim)
    dma = pltpu.SemaphoreType.DMA
    bf16, f32 = jnp.bfloat16, jnp.float32
    blocks = (chunks, chips, block, CHUNK)
    return pl.pallas_call(
        functools.partial(exchange_kernel, chips, held, tall, chans),
        in_specs=[hbm] * 9 + [whole(a) for a in args[9:]],
        out_specs=[hbm] * 4,
        out_shape=[
            jax.ShapeDtypeStruct((rows, modes, cells), bf16),
            jax.ShapeDtypeStruct((rows, modes, cells), bf16),
            jax.ShapeDtypeStruct((2, 3 * half, half), bf16),
            jax.ShapeDtypeStruct((2, 2 * half, half), bf16),
        ],
        scratch_shapes=[
            pltpu.VMEM((2, rows, width, CHUNK), bf16),
            pltpu.VMEM((rows, modes, CHUNK), bf16),
            pltpu.VMEM((rows, modes, CHUNK), bf16),
            pltpu.VMEM((chunks, 2, chips * block, CHUNK), f32),
            pltpu.VMEM((chunks, chips * block, CHUNK), f32),
            pltpu.VMEM(blocks, bf16),
            pltpu.VMEM(blocks, bf16),
            pltpu.VMEM(blocks, bf16),
            pltpu.VMEM((chunks, 2) + blocks[1:], bf16),
            pltpu.VMEM((chunks, rows, modes, CHUNK), bf16),
            pltpu.VMEM((chunks, rows, modes, CHUNK), bf16),
            pltpu.VMEM((2 * chans - 1, size, 128), f32),
            pltpu.VMEM((2, 3 * half, half), bf16),
            pltpu.VMEM((2, 2 * half, half), bf16),
            pltpu.VMEM(press_all.shape[1:], bf16),
            pltpu.VMEM(grow_all.shape[1:], bf16),
            *[pltpu.VMEM(a.shape, a.dtype) for a in args[3:9]],
            dma((chunks, 4)),
            dma((8,)),
            dma((chunks,)),
            dma((chunks,)),
            dma((chunks, chips - 1)),
            dma((chunks, chips - 1)),
            dma((chunks, chips - 1)),
            dma((chunks, chips - 1)),
            dma((chunks, chips)),
            dma((chunks, chips)),
            dma((chunks, 2)),
            dma((2,)),
        ],
        compiler_params=pltpu.CompilerParams(collective_id=5, has_side_effects=True, vmem_limit_bytes=58 * MIB),
    )(*args)


def finish_kernel(chans, u_ref, high_ref, low_ref, basis_ref, local_ref, depth_ref, out_ref, *rhs):
    rows, width, cells = u_ref.shape
    half = cells // 2
    modes = high_ref.shape[1]

    @pl.when(pl.program_id(0) == 0)
    def _():
        for r in rhs:
            r[:, 4 * modes :, :] = local_ref[...]

    def first_layer(row):
        high, low = high_ref[row], low_ref[row]
        parts = []
        for side in range(2):
            lanes = slice(side * half, (side + 1) * half)
            for k, x in enumerate((high, low, high, low)):
                rhs[row][side, modes * k : modes * (k + 1), :] = x[:, lanes]
            u = u_ref[row, :, lanes]
            h = dot(jnp.concatenate([basis_ref[...], u, u], axis=1), rhs[row][side])
            wide = u.astype(jnp.float32)
            parts.append((turn(wide, chans) if side else wide) + act(h))
        return parts

    def second_layer(row, first):
        mixes = []
        for side, x in enumerate((first[0] + first[1], first[0] - first[1])):
            high, low = halves(x)
            mixes.append(dot(jnp.concatenate([high, low, high], axis=1), depth_ref[side]))
        upper = first[1] + act(mixes[0] - mixes[1])
        out_ref[row, :, :half] = (first[0] + act(mixes[0] + mixes[1])).astype(out_ref.dtype)
        out_ref[row, :, half:] = turn(upper, chans).astype(out_ref.dtype)

    firsts = [first_layer(0)]
    for row in range(rows):
        if row + 1 < rows:
            firsts.append(first_layer(row + 1))
        second_layer(row, firsts[row])


def finish(field, high, low, basis, local, depth, chans):
    rows, width, cells = field.shape
    modes = high.shape[1]
    step = math.gcd(rows, 2)
    whole = lambda a: pl.BlockSpec(a.shape, lambda i: (0,) * a.ndim)
    block = pl.BlockSpec((step, width, cells), lambda i: (i, 0, 0))
    thin = pl.BlockSpec((step, modes, cells), lambda i: (i, 0, 0))
    return pl.pallas_call(
        functools.partial(finish_kernel, chans),
        grid=(rows // step,),
        in_specs=[block, thin, thin, whole(basis), whole(local), whole(depth)],
        out_specs=block,
        out_shape=jax.ShapeDtypeStruct(field.shape, jnp.bfloat16),
        scratch_shapes=[pltpu.VMEM((2, 4 * modes + cells, cells // 2), jnp.bfloat16)] * step,
        compiler_params=pltpu.CompilerParams(vmem_limit_bytes=56 * MIB),
        cost_estimate=pl.CostEstimate(
            flops=2 * rows * width * cells * (3 * cells),
            bytes_accessed=4 * rows * width * cells,
            transcendentals=2 * rows * width * cells,
        ),
    )(field, high, low, basis, local, depth)


def stack_halves(x, order, axis):
    pair = np_halves(np.asarray(x, dtype=np.float32))
    return np.concatenate([pair[k] for k in order], axis=axis)


def shards_chips(devices, factors, field, lat_modes, lat_gains, lat_local, depth_modes, depth_local):
    rows, width_y, cells = field.shape
    modes_x, chans, _ = lat_modes.shape
    modes_y = lat_gains.shape[0]
    modes_z = depth_modes.shape[0]
    depth = cells // chans
    chips = devices // 2
    held = modes_y // devices
    basis_y = cosine_basis(width_y, modes_y)
    basis_z = cosine_basis(depth, modes_z)
    left, right = factors
    rank = left.shape[2]
    lead = lead_rows(held, rank)
    tall, block, each = held * rank, held * (rank + lead), 16 // held

    slots = [q * rank + j for q in range(held) for j in range(rank)]
    slots = np.array(slots + [q * rank + j for q in range(held) for j in range(lead)])
    full = (np.arange(block) < tall).astype(np.float32)

    own = right.reshape(chips, rank, 2, rows).transpose(0, 2, 1, 3).reshape(devices, rank, rows)
    kron = np.einsum("djx,qr->dqjxr", own, np.eye(16)).reshape(devices, each, tall, rows * 16)
    kron = kron[:, :, slots].reshape(devices, each * block, rows * 16)
    press = stack_halves(kron, (0, 0, 1), 2)
    high, low = np_halves(np.float32(0.5 * kron.transpose(0, 2, 1)))
    low = (low.astype(np.float32) * np.tile(full, each)).astype(jnp.bfloat16)
    grow = np.concatenate([high, low], axis=2)

    sides = np.einsum("ipj,qr->qpirj", left, np.eye(held)).reshape(held * modes_x, chips, tall)
    flat = np.float32(sides[:, :, slots].reshape(held * modes_x, chips * block))
    high, low = np_halves(flat)
    low = (low.astype(np.float32) * np.tile(full, chips)).astype(jnp.bfloat16)
    front = np.concatenate([high, low], axis=1)
    back = stack_halves(flat.T, (0, 0, 1), 1)
    front_y = stack_halves(basis_y, (0, 1), 0)
    back_y = stack_halves(basis_y.T, (0, 0, 1, 1), 1)

    places = np.arange(chans)
    shift = np.arange(2 * chans - 1) - (chans - 1)
    pick = (places[:, None, None, None] == (places[None, None, None, :] + shift[None, None, :, None])) & (
        places[None, :, None, None] == places[None, None, None, :]
    )
    picks = np.tile(pick.reshape(chans * chans, 2 * chans - 1, chans), (1, 1, 128 // chans))
    picks = picks.reshape(chans * chans, -1).astype(jnp.bfloat16)

    half = depth // 2
    folds = np.stack([np.kron(basis_z[side::2, :half].T, np.eye(chans)) for side in range(2)]).astype(np.float32)
    kinds = np.eye(modes_z)
    sides_z = np.stack([np.kron(kinds[side::2], np.eye(chans)) for side in range(2)]).astype(np.float32)
    spread8 = np.tile(np.eye(chans, dtype=np.float32), (1, modes_z // 2))
    spread16 = np.tile(np.eye(chans, dtype=np.float32), (1, half))

    tables = [press, grow, front, back, picks, folds, folds.transpose(0, 2, 1).copy(), sides_z]
    args = [field] + [jnp.asarray(a) for a in tables] + [jnp.asarray(front_y), lat_gains.T]
    args += [lat_modes.transpose(1, 2, 0).reshape(chans * chans, modes_x)]
    args += [jnp.asarray(a) for a in (spread8, spread16, spread16.T.copy())]
    args += [depth_modes.reshape(modes_z * chans, chans), depth_local, lat_local]
    high, low, depth_ops, local_ops = exchange(chips, held, tall, block, chans, *args)
    return finish(field, high, low, jnp.asarray(back_y), local_ops, depth_ops, chans)


def lead_rows(held, rank):
    lead = LEAD
    while held * (rank + lead) % 16:
        lead += 1
    return lead


def wide_basis(length, modes):
    order = np.arange(modes, dtype=np.float64)[:, None]
    place = np.arange(length, dtype=np.float64)[None, :]
    scales = np.where(order == 0.0, math.sqrt(1.0 / length), math.sqrt(2.0 / length))
    return np.cos(math.pi * order * (place + 0.5) / length) * scales


def shards(field, lat_modes, lat_gains, lat_local, depth_modes, depth_local):
    devices = lax.axis_size("lat")
    rows, _, cells = field.shape
    modes_x, chans, _ = lat_modes.shape
    modes_y, modes_z = lat_gains.shape[0], depth_modes.shape[0]
    args = (field, lat_modes, lat_gains, lat_local, depth_modes, depth_local)
    fits = devices % 2 == 0 and modes_y % (2 * devices) == 0 and modes_y % 64 == 0 and 16 % (modes_y // devices) == 0
    fits = fits and rows % 8 == 0 and cells % (4 * CHUNK) == 0 and chans * modes_z == 256 and cells == 512 and chans * chans == 256
    if fits:
        held = modes_y // devices
        factors = window_factors(wide_basis(rows * devices, modes_x), devices // 2, 1)
        rank = factors[0].shape[2]
        if rank >= lead_rows(held, rank):
            return shards_chips(devices, factors, *args)
    return shards_rows(*args)


def solution(mesh):
    placed = (P(("group", "lat"), None, None), P(), P(), P(), P(), P())
    return jax.shard_map(
        shards,
        mesh=mesh,
        in_specs=placed,
        out_specs=P(("group", "lat"), None, None),
        check_vma=False,
    )
```

```python
import functools
import math

import jax
import jax.numpy as jnp
import numpy as np
from jax import lax
from jax.experimental import pallas as pl
from jax.experimental.pallas import tpu as pltpu
from jax.sharding import PartitionSpec as P

LINK = jnp.float16
SCALE_OUT = 256.0
SCALE_BACK = 1.0 / 16.0
K0 = math.sqrt(2.0 / math.pi)
K1 = K0 * 0.044715
MIB = 1 << 20


def cosine_basis(length, modes):
    order = np.arange(modes, dtype=np.float64)[:, None]
    place = np.arange(length, dtype=np.float64)[None, :]
    scales = np.where(order == 0.0, math.sqrt(1.0 / length), math.sqrt(2.0 / length))
    return (np.cos(math.pi * order * (place + 0.5) / length) * scales).astype(np.float32)


def halves(x):
    high = jnp.asarray(x).astype(jnp.bfloat16)
    low = (x - high.astype(jnp.float32)).astype(jnp.bfloat16)
    return high, low


def outer_halves(x):
    high = lax.reduce_precision(x, 8, 7)
    return high.astype(jnp.bfloat16), (x - high).astype(jnp.bfloat16)


def np_halves(x):
    high = np.asarray(x, dtype=jnp.bfloat16)
    low = np.asarray(x - high.astype(np.float32), dtype=jnp.bfloat16)
    return high, low


def dot(a, b):
    return jnp.dot(a, b, preferred_element_type=jnp.float32)


def gelu(x):
    half = 0.5 * x
    return half + half * jnp.tanh(x * (K0 + K1 * (x * x)))


def forward_kernel(basis_ref, u_ref, out_ref):
    modes = out_ref.shape[1]

    def body(row, carry):
        both = dot(basis_ref[...], u_ref[row])
        out_ref[row] = (both[:modes] + both[modes:]) * SCALE_OUT
        return carry

    lax.fori_loop(0, u_ref.shape[0], body, 0)


def forward(field, basis, start, rows):
    _, width, cells = field.shape
    modes = basis.shape[0] // 2
    step = math.gcd(rows, 4)
    return pl.pallas_call(
        forward_kernel,
        grid=(rows // step,),
        in_specs=[
            pl.BlockSpec(basis.shape, lambda i: (0, 0)),
            pl.BlockSpec((step, width, cells), lambda i: (i + start // step, 0, 0)),
        ],
        out_specs=pl.BlockSpec((step, modes, cells), lambda i: (i, 0, 0)),
        out_shape=jax.ShapeDtypeStruct((rows, modes, cells), jnp.float32),
        compiler_params=pltpu.CompilerParams(vmem_limit_bytes=40 * MIB),
        cost_estimate=pl.CostEstimate(
            flops=4 * rows * modes * width * cells,
            bytes_accessed=rows * cells * (2 * width + 4 * modes),
            transcendentals=0,
        ),
    )(basis, field)


def middle_kernel(chunks, chans, *refs):
    g_refs = refs[:chunks]
    f_refs = refs[chunks : 2 * chunks]
    b_refs = refs[2 * chunks : 3 * chunks]
    gain_ref, diag_ref = refs[3 * chunks : 3 * chunks + 2]
    out_refs = refs[3 * chunks + 2 :]
    modes = diag_ref.shape[1]
    coef = None
    for g_ref, f_ref in zip(g_refs, f_refs):
        high, low = halves(g_ref[0])
        both = dot(f_ref[...], high)
        part = both[:modes] + both[modes:] + dot(f_ref[:modes], low)
        coef = part if coef is None else coef + part
    coef = coef * gain_ref[0]
    tiles = []
    for lane in range(0, coef.shape[1], 128):
        tile = coef[:, lane : lane + 128]
        total = tile * diag_ref[chans - 1]
        for at in range(2 * chans - 1):
            shift = at - (chans - 1)
            if shift != 0:
                total += pltpu.roll(tile, (-shift) % 128, 1) * diag_ref[at]
        tiles.append(total)
    mixed = jnp.concatenate(tiles, axis=1) if len(tiles) > 1 else tiles[0]
    high, low = halves(mixed)
    stacked = jnp.concatenate([high, low, high], axis=0)
    for b_ref, out_ref in zip(b_refs, out_refs):
        out_ref[0] = dot(b_ref[...], stacked)


def middle(gathered, fronts, backs, gains, diags):
    chunks = len(gathered)
    count, length, width = gathered[0].shape
    modes = diags.shape[1]
    chans = (diags.shape[0] + 1) // 2
    whole = lambda a: pl.BlockSpec(a.shape, lambda i: (0,) * a.ndim)
    block = pl.BlockSpec((1, length, width), lambda i: (i, 0, 0))
    return pl.pallas_call(
        functools.partial(middle_kernel, chunks, chans),
        grid=(count,),
        in_specs=[block] * chunks
        + [whole(a) for a in fronts]
        + [whole(a) for a in backs]
        + [pl.BlockSpec((1, 1, width), lambda i: (i, 0, 0)), whole(diags)],
        out_specs=[block] * chunks,
        out_shape=[jax.ShapeDtypeStruct((count, length, width), jnp.float32)] * chunks,
        compiler_params=pltpu.CompilerParams(vmem_limit_bytes=40 * MIB),
    )(*gathered, *fronts, *backs, gains, diags)


def tail_kernel(piece, u_ref, back_ref, basis_ref, local_ref, depth_ref, *refs):
    out_ref = refs[-1]
    _, width, cells = u_ref.shape
    block = local_ref.shape[1]
    high, low = halves(back_ref[0])
    stacked = jnp.concatenate([high, low, high], axis=0)

    def body(at, carry):
        rows = pl.ds(pl.multiple_of(at * piece, piece), piece)
        u = u_ref[0, rows, :]
        spect = dot(basis_ref[rows, :], stacked)
        parts = []
        for lane in range(0, cells, block):
            tile = u[:, lane : lane + block]
            parts.append(dot(tile, local_ref[0]) + dot(tile, local_ref[1]))
        local = jnp.concatenate(parts, axis=1) if len(parts) > 1 else parts[0]
        first = u.astype(jnp.float32) + gelu(spect + local)
        high1, low1 = halves(first)
        mix = dot(high1, depth_ref[0]) + dot(low1, depth_ref[0]) + dot(high1, depth_ref[1])
        out_ref[0, rows, :] = (first + gelu(mix)).astype(out_ref.dtype)
        return carry

    lax.fori_loop(0, width // piece, body, 0)


def tail(field, back, basis, local, depth, previous, start):
    rows, modes, cells = back.shape
    width = field.shape[1]
    whole = lambda a: pl.BlockSpec(a.shape, lambda i: (0,) * a.ndim)
    operands = [field, back, basis, local, depth]
    specs = [
        pl.BlockSpec((1, width, cells), lambda i: (i + start, 0, 0)),
        pl.BlockSpec((1, modes, cells), lambda i: (i, 0, 0)),
        whole(basis),
        whole(local),
        whole(depth),
    ]
    aliases = {}
    if previous is not None:
        aliases = {len(operands): 0}
        operands.append(previous)
        specs.append(pl.BlockSpec(memory_space=pl.ANY))
    return pl.pallas_call(
        functools.partial(tail_kernel, math.gcd(width, 256)),
        grid=(rows,),
        in_specs=specs,
        out_specs=pl.BlockSpec((1, width, cells), lambda i: (i + start, 0, 0)),
        out_shape=jax.ShapeDtypeStruct(field.shape, jnp.bfloat16),
        input_output_aliases=aliases,
        compiler_params=pltpu.CompilerParams(vmem_limit_bytes=48 * MIB),
        cost_estimate=pl.CostEstimate(
            flops=2 * rows * width * cells * (4 * cells),
            bytes_accessed=4 * rows * width * cells,
            transcendentals=2 * rows * width * cells,
        ),
    )(*operands)


def block_diagonal(small, size):
    chans = small.shape[0]
    copies = size // chans
    ids = np.arange(size) // chans
    mask = (ids[:, None] == ids[None, :]).astype(np.float32)
    return jnp.tile(small, (copies, copies)) * mask


def shards_rows(field, lat_modes, lat_gains, lat_local, depth_modes, depth_local):
    highest = lax.Precision.HIGHEST
    devices = lax.axis_size("lat")
    rows_dev, width_y, cells = field.shape
    modes_x, chans, _ = lat_modes.shape
    modes_y = lat_gains.shape[0]
    modes_z = depth_modes.shape[0]
    depth = cells // chans
    width_x = rows_dev * devices
    chunks = 2 if rows_dev % 16 == 0 else 1
    rows = rows_dev // chunks
    splits = max(1, devices // modes_y)
    held = modes_y * splits // devices
    span = cells // splits
    basis_x = cosine_basis(width_x, modes_x)
    basis_y = cosine_basis(width_y, modes_y)
    basis_z = cosine_basis(depth, modes_z)

    high_y, low_y = np_halves(basis_y)
    front_y = jnp.asarray(np.concatenate([high_y, low_y], axis=0))
    back_y = jnp.asarray(np.concatenate([high_y, high_y, low_y], axis=0).T.copy())
    fronts, backs = [], []
    for chunk in range(chunks):
        part = basis_x.reshape(modes_x, devices, chunks, rows)[:, :, chunk].reshape(modes_x, -1)
        high_x, low_x = np_halves(part)
        fronts.append(jnp.asarray(np.concatenate([high_x, low_x], axis=0)))
        backs.append(jnp.asarray(np.concatenate([high_x, high_x, low_x], axis=0).T.copy()))

    gathered = []
    for chunk in range(chunks):
        coef_y = forward(field, front_y, chunk * rows, rows)
        sent = coef_y.astype(LINK).reshape(rows, modes_y, splits, span)
        sent = sent.transpose(1, 2, 0, 3).reshape(modes_y * splits, rows, span)
        gathered.append(lax.all_to_all(sent, "lat", split_axis=0, concat_axis=0, tiled=True))

    shift = np.arange(2 * chans - 1)[:, None, None] - (chans - 1)
    places = np.arange(chans)
    pick = (places[None, :, None] == places[None, None, :] + shift).astype(np.float32)
    diags = jnp.sum(lat_modes[None] * pick[:, None], axis=2)
    diags = jnp.tile(diags, (1, 1, 128 // chans))
    me = lax.axis_index("lat")
    gain_rows = lax.dynamic_slice_in_dim(lat_gains, me * held // splits, held, 0)
    gain_rows = jnp.tile(gain_rows * (SCALE_BACK / SCALE_OUT), (1, span // chans))[:, None, :]

    spread = np.kron(basis_z.T, np.eye(chans, dtype=np.float32))
    ids = np.arange(modes_z * chans) // chans
    mask = (ids[:, None] == ids[None, :]).astype(np.float32)
    mixers = jnp.tile(depth_modes.reshape(modes_z * chans, chans), (1, modes_z)) * mask
    inner = jnp.dot(mixers, spread.T, precision=highest)
    whole = jnp.dot(spread, inner, precision=highest) + block_diagonal(depth_local, cells)
    depth_pair = jnp.stack(outer_halves(whole))
    local_pair = jnp.stack(outer_halves(block_diagonal(lat_local, math.gcd(cells, 256))))

    received = []
    for got in gathered:
        got = got.reshape(devices, held, rows, span).transpose(1, 0, 2, 3).astype(jnp.float32)
        received.append(got.reshape(held, devices * rows, span))
    mixed = middle(received, fronts, backs, gain_rows, diags)
    returned = []
    for part in mixed:
        part = part.astype(LINK).reshape(held, devices, rows, span).transpose(1, 0, 2, 3)
        part = part.reshape(devices * held, rows, span)
        returned.append(lax.all_to_all(part, "lat", split_axis=0, concat_axis=0, tiled=True))
    out = None
    for chunk, part in enumerate(returned):
        part = part.reshape(modes_y, splits, rows, span).transpose(2, 0, 1, 3)
        part = part.reshape(rows, modes_y, cells).astype(jnp.float32) * (1.0 / SCALE_BACK)
        out = tail(field, part, back_y, local_pair, depth_pair, out, chunk * rows)
    return out

LINK_OUT = 64.0
LINK_BACK = 1.0 / 32.0
C0 = 2.0 * K0
C1 = 8.0 * K1


def act(h):
    return h + h * jnp.tanh(h * (C0 + C1 * (h * h)))


def window_factors(basis, windows, fine):
    modes = basis.shape[0]
    blocks = basis.reshape(modes, windows, -1).transpose(1, 0, 2)
    left, sizes, right = np.linalg.svd(blocks, full_matrices=False)
    left = left * sizes[:, None, :]
    top = np.abs(basis).max()
    rank = fine
    while rank < sizes.shape[1]:
        product = left[:, :, :rank] @ right[:, :rank]
        if np.abs(product - blocks).max() <= 2.0 ** -23 * top:
            break
        rank += fine
    return left[:, :, :rank], right[:, :rank]


def turn(x, unit):
    place = lax.broadcasted_iota(jnp.int32, (x.shape[0], 128), 1)
    place = (128 - unit - place // unit * unit) + place % unit
    tiles = [jnp.take_along_axis(x[:, at : at + 128], place, axis=1) for at in range(0, x.shape[1], 128)]
    return jnp.concatenate(tiles[::-1], axis=1)


LEAD = 9
CHUNK = 128
ORDER = (0, 3, 1, 2)


def exact(a, b):
    return jnp.dot(a, b, preferred_element_type=jnp.float32, precision=lax.Precision.HIGHEST)


def turned_dot(a, b, precision=None):
    return lax.dot_general(a, b, (((0,), (0,)), ((), ())), precision=precision, preferred_element_type=jnp.float32)


def quarter_mask(size, unit):
    half = size // unit // 2
    row = lax.broadcasted_iota(jnp.int32, (size, size), 0) // unit
    lane = lax.broadcasted_iota(jnp.int32, (size, size), 1) // unit
    return (row == jnp.where(lane < half, lane, 3 * half - 1 - lane)).astype(jnp.float32)


def block_mask(size, unit, flip):
    row = lax.broadcasted_iota(jnp.int32, (size, size), 0) // unit
    lane = lax.broadcasted_iota(jnp.int32, (size, size), 1) // unit
    return (row == (size // unit - 1 - lane if flip else lane)).astype(jnp.float32)


def exchange_kernel(chips, held, tall, chans, *refs):
    field, press_all, grow_all, front_in, back_in, picks_in, folds_in, folds_t_in, sides_in = refs[:9]
    basis, gains, modes_in, spread8, spread16, spread_t, depth_in, depth_local, lat_local, synth = refs[9:19]
    high_out, low_out, depth_out, local_out, early_out = refs[19:24]
    (u, highs, lows, part, fresh, send, land, reply, home, wide_high, wide_low, diags, depth_ops, local_ops, firsts, rhs) = refs[24:40]
    press, grow, front, back, picks, folds, folds_t, sides = refs[40:48]
    load_sem, table_sem, pair_send, pair_recv, out_send, out_recv, in_send, in_recv, hand_send, hand_recv, store_sem, ops_sem, again_sem, early_sem = refs[48:]
    rows, width, cells = field.shape
    modes = basis.shape[0] // 2
    chunks = cells // CHUNK
    block = send.shape[2]
    mesh_ids = pl.DeviceIdType.MESH
    me = lax.axis_index("lat")
    chip, core = me // 2, lax.rem(me, 2)
    other = chip * 2 + 1 - core
    subs = 4
    span = rows // subs

    def load(ch, sub):
        take = pl.ds(sub * span, span)
        return pltpu.make_async_copy(
            field.at[take, :, pl.ds(ORDER[ch] * CHUNK, CHUNK)], u.at[ch % 2, take], load_sem.at[ch, sub]
        )

    def tables():
        sources = (press_all.at[me], grow_all.at[me], front_in, back_in, picks_in, folds_in, folds_t_in, sides_in)
        targets = (press, grow, front, back, picks, folds, folds_t, sides)
        pairs = enumerate(zip(sources, targets))
        return [pltpu.make_async_copy(source, target, table_sem.at[k]) for k, (source, target) in pairs]

    for sub in range(subs):
        load(0, sub).start()
    tables()[0].start()
    for sub in range(subs):
        load(1, sub).start()
    for copy in tables()[1:]:
        copy.start()

    barrier = pltpu.get_barrier_semaphore()
    for off in range(1, chips):
        peer = lax.rem(chip + off, chips) * 2 + core
        pl.semaphore_signal(barrier, inc=1, device_id={"lat": peer}, device_id_type=mesh_ids)
    pl.semaphore_signal(barrier, inc=1, device_id={"lat": other}, device_id_type=mesh_ids)

    def pair_copy(ch):
        return pltpu.make_async_remote_copy(
            src_ref=part.at[ch, 1 - core],
            dst_ref=fresh.at[ch],
            send_sem=pair_send.at[ch],
            recv_sem=pair_recv.at[ch],
            device_id={"lat": other},
            device_id_type=mesh_ids,
        )

    def chip_copy(source, target, send_sems, recv_sems, ch, off):
        to = lax.rem(chip + off, chips)
        return pltpu.make_async_remote_copy(
            src_ref=source.at[ch, to],
            dst_ref=target.at[chip],
            send_sem=send_sems.at[ch, off - 1],
            recv_sem=recv_sems.at[ch, off - 1],
            device_id={"lat": to * 2 + core},
            device_id_type=mesh_ids,
        )

    def out_copy(ch, off):
        return chip_copy(send, land.at[ch], out_send, out_recv, ch, off)

    def in_copy(ch, off):
        return chip_copy(reply, home.at[ch, core], in_send, in_recv, ch, off)

    def hand_copy(ch, off):
        slot = lax.rem(chip + chips - off, chips)
        return pltpu.make_async_remote_copy(
            src_ref=home.at[ch, core, slot],
            dst_ref=home.at[ch, core, slot],
            send_sem=hand_send.at[ch, off],
            recv_sem=hand_recv.at[ch, off],
            device_id={"lat": other},
            device_id_type=mesh_ids,
        )

    def analyse(ch):
        for sub in range(subs):
            load(ch, sub).wait()

            def body(k, carry):
                x = sub * span + 2 * k
                pair = jnp.concatenate([u[ch % 2, x], u[ch % 2, x + 1]], axis=1)
                both = dot(basis[...], pair)
                high, low = halves(both[:modes] + both[modes:])
                for at in range(2):
                    highs[x + at] = high[:, at * CHUNK : (at + 1) * CHUNK]
                    lows[x + at] = low[:, at * CHUNK : (at + 1) * CHUNK]
                return carry

            lax.fori_loop(0, span // 2, body, 0, unroll=True)
        if ch + 2 < chunks:
            for sub in range(subs):
                load(ch + 2, sub).start()
        if ch == 0:
            tables()[0].wait()
        count = press.shape[0]
        for group in range(0, modes // 16, 2):
            stacks = []
            for g in (group, group + 1):
                take = slice(16 * g, 16 * g + 16)
                high = highs[:, take, :].reshape(rows * 16, CHUNK)
                low = lows[:, take, :].reshape(rows * 16, CHUNK)
                stacks.append(jnp.concatenate([high, low, high], axis=0))
            product = dot(press[...], jnp.concatenate(stacks, axis=1))
            half, within = divmod(group, modes // 32)
            for at in range(2):
                part[ch, half, count * (within + at) : count * (within + at + 1), :] = product[:, at * CHUNK : (at + 1) * CHUNK]

    def spill(value, target, ch):
        high, low = halves(value)
        place = lax.broadcasted_iota(jnp.int32, value.shape, 0) % block
        target[ch] = jnp.where(place < tall, high, low).reshape(chips, block, CHUNK)

    def emit(ch):
        pair_copy(ch).wait_recv()
        spill(part[ch, core] + fresh[ch], send, ch)
        for off in range(1, chips):
            out_copy(ch, off).start()
        land[ch, chip] = send[ch, chip]

    def prepare():
        rest, total = modes_in[...], None
        for _ in range(3):
            term = rest.astype(jnp.bfloat16)
            rest = rest - term.astype(jnp.float32)
            product = turned_dot(term, picks[...])
            total = product if total is None else total + product
        for at in range(2 * chans - 1):
            diags[at] = total[:, at * 128 : (at + 1) * 128]
        half = folds.shape[1]
        local = exact(exact(spread_t[...], depth_local[...]), spread16[...]) * block_mask(half, chans, False)
        for side in range(2):
            mixer = exact(exact(sides[side], depth_in[...]), spread8[...]) * block_mask(folds.shape[2], chans, False)
            whole = 0.5 * exact(exact(folds[side], mixer), folds_t[side]) + 0.25 * local
            high, low = halves(whole)
            for at, x in enumerate((high, high, low)):
                depth_ops[side, at * half : (at + 1) * half, :] = x
        spot = exact(exact(spread_t[...], lat_local[...]), spread16[...]) * 0.5
        high, low = halves(spot * quarter_mask(half, chans))
        local_ops[:half, :] = high
        local_ops[half:, :] = low
        for slot in range(2):
            rhs[slot, 4 * modes : 4 * modes + half, :] = high
            rhs[slot, 4 * modes + half :, :] = low

    def ops_copies():
        return (
            pltpu.make_async_copy(depth_ops, depth_out, ops_sem.at[0]),
            pltpu.make_async_copy(local_ops, local_out, ops_sem.at[1]),
        )

    first_q = core * (modes // 2) + chip * held

    def blend(ch):
        for off in range(1, chips):
            out_copy(ch, off).wait_recv()
        values = land[ch].reshape(chips * block, CHUNK)
        coef = dot(front[...], jnp.concatenate([values, values], axis=0))
        scale = turned_dot(gains[...], spread8[...], lax.Precision.HIGHEST)
        size = diags.shape[1]
        upper, lower = [], []
        for q in range(held):
            tile = coef[q * size : (q + 1) * size] * gains_row(scale, q)
            total = tile * diags[chans - 1]
            for at in range(2 * chans - 1):
                shift = at - (chans - 1)
                if shift != 0:
                    total += pltpu.roll(tile, (-shift) % 128, 1) * diags[at]
            if 2 * ORDER[ch] >= chunks:
                total = turn(total, chans)
            high, low = halves(total)
            upper.append(high)
            lower.append(low)
        spill(dot(back[...], jnp.concatenate(upper + lower + upper, axis=0)), reply, ch)
        for off in range(1, chips):
            in_copy(ch, off).start()
        home[ch, core, chip] = reply[ch, chip]
        hand_copy(ch, 0).start()

    def gains_row(scale, q):
        at = lax.broadcasted_iota(jnp.int32, scale.shape, 0)
        return jnp.sum(jnp.where(at == first_q + q, scale, 0.0), axis=0, keepdims=True)

    def hand(ch):
        for off in range(1, chips):
            in_copy(ch, off).wait_recv()
            hand_copy(ch, off).start()

    def store_copies(ch):
        lanes = pl.ds((ch - 2) * CHUNK, CHUNK)
        return (
            pltpu.make_async_copy(wide_high.at[ch], high_out.at[:, :, lanes], store_sem.at[ch - 2, 0]),
            pltpu.make_async_copy(wide_low.at[ch], low_out.at[:, :, lanes], store_sem.at[ch - 2, 1]),
        )

    def again(ch):
        return pltpu.make_async_copy(field.at[:, :, pl.ds(ORDER[ch] * CHUNK, CHUNK)], u.at[ch], again_sem.at[ch])

    def early_copy(x, slot):
        return pltpu.make_async_copy(firsts.at[slot], early_out.at[x], early_sem.at[slot])

    def early(start, stop):
        def body(k, carry):
            for slot in range(2):
                x = 2 * k + slot

                @pl.when(k > 0)
                def _():
                    early_copy(x - 2, slot).wait()

                high = jnp.concatenate([wide_high[0, x], wide_high[1, x]], axis=1)
                low = jnp.concatenate([wide_low[0, x], wide_low[1, x]], axis=1)
                for at, part_rows in enumerate((high, low, high, low)):
                    rhs[slot, at * modes : (at + 1) * modes, :] = part_rows
                both = jnp.concatenate([u[0, x], u[1, x]], axis=1)
                h = dot(jnp.concatenate([synth[...], both, both], axis=1), rhs[slot])
                wide = both.astype(jnp.float32)
                firsts[slot, :, :CHUNK] = wide[:, :CHUNK] + act(h[:, :CHUNK])
                firsts[slot, :, CHUNK:] = turn(wide[:, CHUNK:], chans) + act(h[:, CHUNK:])
                early_copy(x, slot).start()
            return carry

        lax.fori_loop(start // 2, stop // 2, body, 0)

    def expand(ch):
        for off in range(chips):
            hand_copy(ch, off).wait_recv()
        each = 16 // held
        for group in range(0, modes // 16, 2):
            stacks = []
            for g in (group, group + 1):
                half, within = divmod(g, modes // 32)
                take = slice(each * within, each * (within + 1))
                values = home[ch, half, take].reshape(each * block, CHUNK)
                stacks.append(jnp.concatenate([values, values], axis=0))
            high, low = halves(dot(grow[...], jnp.concatenate(stacks, axis=1)))
            for at in range(2):
                take = slice(16 * (group + at), 16 * (group + at + 1))
                lanes = slice(at * CHUNK, (at + 1) * CHUNK)
                wide_high[ch, :, take, :] = high[:, lanes].reshape(rows, 16, CHUNK)
                wide_low[ch, :, take, :] = low[:, lanes].reshape(rows, 16, CHUNK)
        if ch >= 2:
            for copy in store_copies(ch):
                copy.start()

    analyse(0)
    pl.semaphore_wait(barrier, chips)
    pair_copy(0).start()
    emit(0)
    for ch in range(1, chunks):
        analyse(ch)
        pair_copy(ch).start()
        if ch > 1:
            emit(ch - 1)
    again(0).start()
    again(1).start()
    emit(chunks - 1)
    for copy in tables()[1:]:
        copy.wait()
    prepare()
    for copy in ops_copies():
        copy.start()
    for ch in range(chunks):
        blend(ch)
    hand(0)
    hand(1)
    expand(0)
    expand(1)
    again(0).wait()
    again(1).wait()
    early(0, rows // 2)
    hand(2)
    early(rows // 2, rows)
    hand(3)
    expand(2)
    expand(3)
    for slot in range(2):
        early_copy(rows - 2 + slot, slot).wait()
    for ch in range(chunks):
        pair_copy(ch).wait_send()
        for off in range(1, chips):
            out_copy(ch, off).wait_send()
            in_copy(ch, off).wait_send()
        for off in range(chips):
            hand_copy(ch, off).wait_send()
    for ch in range(2, chunks):
        for copy in store_copies(ch):
            copy.wait()
    for copy in ops_copies():
        copy.wait()


def exchange(chips, held, tall, block, chans, *args):
    field, press_all, grow_all = args[:3]
    basis, gains = args[9:11]
    rows, width, cells = field.shape
    modes = basis.shape[0] // 2
    chunks = cells // CHUNK
    half = cells // 2
    size = args[11].shape[1]
    hbm = pl.BlockSpec(memory_space=pl.ANY)
    whole = lambda a: pl.BlockSpec(a.shape, lambda: (0,) * a.ndim)
    dma = pltpu.SemaphoreType.DMA
    bf16, f32 = jnp.bfloat16, jnp.float32
    blocks = (chunks, chips, block, CHUNK)
    return pl.pallas_call(
        functools.partial(exchange_kernel, chips, held, tall, chans),
        in_specs=[hbm] * 9 + [whole(a) for a in args[9:]],
        out_specs=[hbm] * 5,
        out_shape=[
            jax.ShapeDtypeStruct((rows, modes, half), bf16),
            jax.ShapeDtypeStruct((rows, modes, half), bf16),
            jax.ShapeDtypeStruct((2, 3 * half, half), bf16),
            jax.ShapeDtypeStruct((2 * half, half), bf16),
            jax.ShapeDtypeStruct((rows, width, half), f32),
        ],
        scratch_shapes=[
            pltpu.VMEM((2, rows, width, CHUNK), bf16),
            pltpu.VMEM((rows, modes, CHUNK), bf16),
            pltpu.VMEM((rows, modes, CHUNK), bf16),
            pltpu.VMEM((chunks, 2, chips * block, CHUNK), f32),
            pltpu.VMEM((chunks, chips * block, CHUNK), f32),
            pltpu.VMEM(blocks, bf16),
            pltpu.VMEM(blocks, bf16),
            pltpu.VMEM(blocks, bf16),
            pltpu.VMEM((chunks, 2) + blocks[1:], bf16),
            pltpu.VMEM((chunks, rows, modes, CHUNK), bf16),
            pltpu.VMEM((chunks, rows, modes, CHUNK), bf16),
            pltpu.VMEM((2 * chans - 1, size, 128), f32),
            pltpu.VMEM((2, 3 * half, half), bf16),
            pltpu.VMEM((2 * half, half), bf16),
            pltpu.VMEM((2, width, half), f32),
            pltpu.VMEM((2, 4 * modes + 2 * half, half), bf16),
            pltpu.VMEM(press_all.shape[1:], bf16),
            pltpu.VMEM(grow_all.shape[1:], bf16),
            *[pltpu.VMEM(a.shape, a.dtype) for a in args[3:9]],
            dma((chunks, 4)),
            dma((8,)),
            dma((chunks,)),
            dma((chunks,)),
            dma((chunks, chips - 1)),
            dma((chunks, chips - 1)),
            dma((chunks, chips - 1)),
            dma((chunks, chips - 1)),
            dma((chunks, chips)),
            dma((chunks, chips)),
            dma((2, 2)),
            dma((2,)),
            dma((2,)),
            dma((2,)),
        ],
        compiler_params=pltpu.CompilerParams(collective_id=5, has_side_effects=True, vmem_limit_bytes=58 * MIB),
    )(*args)


def finish_kernel(chans, u_ref, high_ref, low_ref, early_ref, basis_ref, local_ref, depth_ref, out_ref, *rhs):
    rows, width, cells = u_ref.shape
    half = cells // 2
    modes = high_ref.shape[1]

    @pl.when(pl.program_id(0) == 0)
    def _():
        for r in rhs:
            r[4 * modes :, :] = local_ref[...]

    def first_layer(row):
        high, low = high_ref[row], low_ref[row]
        for k, x in enumerate((high, low, high, low)):
            rhs[row][modes * k : modes * (k + 1), :] = x
        u = u_ref[row, :, CHUNK : CHUNK + half]
        h = dot(jnp.concatenate([basis_ref[...], u, u], axis=1), rhs[row][...])
        wide = u.astype(jnp.float32)
        lower = wide[:, :CHUNK] + act(h[:, :CHUNK])
        upper = turn(wide[:, CHUNK:], chans) + act(h[:, CHUNK:])
        return [
            jnp.concatenate([early_ref[row, :, :CHUNK], lower], axis=1),
            jnp.concatenate([early_ref[row, :, CHUNK:], upper], axis=1),
        ]

    def second_layer(row, first):
        mixes = []
        for side, x in enumerate((first[0] + first[1], first[0] - first[1])):
            high, low = halves(x)
            mixes.append(dot(jnp.concatenate([high, low, high], axis=1), depth_ref[side]))
        upper = first[1] + act(mixes[0] - mixes[1])
        out_ref[row, :, :half] = (first[0] + act(mixes[0] + mixes[1])).astype(out_ref.dtype)
        out_ref[row, :, half:] = turn(upper, chans).astype(out_ref.dtype)

    firsts = [first_layer(0)]
    for row in range(rows):
        if row + 1 < rows:
            firsts.append(first_layer(row + 1))
        second_layer(row, firsts[row])


def finish(field, high, low, early, basis, local, depth, chans):
    rows, width, cells = field.shape
    modes = high.shape[1]
    step = math.gcd(rows, 2)
    whole = lambda a: pl.BlockSpec(a.shape, lambda i: (0,) * a.ndim)
    block = pl.BlockSpec((step, width, cells), lambda i: (i, 0, 0))
    thin = pl.BlockSpec((step, modes, cells // 2), lambda i: (i, 0, 0))
    wide = pl.BlockSpec((step, width, cells // 2), lambda i: (i, 0, 0))
    return pl.pallas_call(
        functools.partial(finish_kernel, chans),
        grid=(rows // step,),
        in_specs=[block, thin, thin, wide, whole(basis), whole(local), whole(depth)],
        out_specs=block,
        out_shape=jax.ShapeDtypeStruct(field.shape, jnp.bfloat16),
        scratch_shapes=[pltpu.VMEM((4 * modes + cells, cells // 2), jnp.bfloat16)] * step,
        compiler_params=pltpu.CompilerParams(vmem_limit_bytes=56 * MIB),
        cost_estimate=pl.CostEstimate(
            flops=2 * rows * width * cells * (3 * cells),
            bytes_accessed=4 * rows * width * cells,
            transcendentals=2 * rows * width * cells,
        ),
    )(field, high, low, early, basis, local, depth)


def stack_halves(x, order, axis):
    pair = np_halves(np.asarray(x, dtype=np.float32))
    return np.concatenate([pair[k] for k in order], axis=axis)


def shards_chips(devices, factors, field, lat_modes, lat_gains, lat_local, depth_modes, depth_local):
    rows, width_y, cells = field.shape
    modes_x, chans, _ = lat_modes.shape
    modes_y = lat_gains.shape[0]
    modes_z = depth_modes.shape[0]
    depth = cells // chans
    chips = devices // 2
    held = modes_y // devices
    basis_y = cosine_basis(width_y, modes_y)
    basis_z = cosine_basis(depth, modes_z)
    left, right = factors
    rank = left.shape[2]
    lead = lead_rows(held, rank)
    tall, block, each = held * rank, held * (rank + lead), 16 // held

    slots = [q * rank + j for q in range(held) for j in range(rank)]
    slots = np.array(slots + [q * rank + j for q in range(held) for j in range(lead)])
    full = (np.arange(block) < tall).astype(np.float32)

    own = right.reshape(chips, rank, 2, rows).transpose(0, 2, 1, 3).reshape(devices, rank, rows)
    kron = np.einsum("djx,qr->dqjxr", own, np.eye(16)).reshape(devices, each, tall, rows * 16)
    kron = kron[:, :, slots].reshape(devices, each * block, rows * 16)
    press = stack_halves(kron, (0, 0, 1), 2)
    high, low = np_halves(np.float32(0.5 * kron.transpose(0, 2, 1)))
    low = (low.astype(np.float32) * np.tile(full, each)).astype(jnp.bfloat16)
    grow = np.concatenate([high, low], axis=2)

    sides = np.einsum("ipj,qr->qpirj", left, np.eye(held)).reshape(held * modes_x, chips, tall)
    flat = np.float32(sides[:, :, slots].reshape(held * modes_x, chips * block))
    high, low = np_halves(flat)
    low = (low.astype(np.float32) * np.tile(full, chips)).astype(jnp.bfloat16)
    front = np.concatenate([high, low], axis=1)
    back = stack_halves(flat.T, (0, 0, 1), 1)
    front_y = stack_halves(basis_y, (0, 1), 0)
    back_y = stack_halves(basis_y.T, (0, 0, 1, 1), 1)

    places = np.arange(chans)
    shift = np.arange(2 * chans - 1) - (chans - 1)
    pick = (places[:, None, None, None] == (places[None, None, None, :] + shift[None, None, :, None])) & (
        places[None, :, None, None] == places[None, None, None, :]
    )
    picks = np.tile(pick.reshape(chans * chans, 2 * chans - 1, chans), (1, 1, 128 // chans))
    picks = picks.reshape(chans * chans, -1).astype(jnp.bfloat16)

    half = depth // 2
    folds = np.stack([np.kron(basis_z[side::2, :half].T, np.eye(chans)) for side in range(2)]).astype(np.float32)
    kinds = np.eye(modes_z)
    sides_z = np.stack([np.kron(kinds[side::2], np.eye(chans)) for side in range(2)]).astype(np.float32)
    spread8 = np.tile(np.eye(chans, dtype=np.float32), (1, modes_z // 2))
    spread16 = np.tile(np.eye(chans, dtype=np.float32), (1, half))

    tables = [press, grow, front, back, picks, folds, folds.transpose(0, 2, 1).copy(), sides_z]
    args = [field] + [jnp.asarray(a) for a in tables] + [jnp.asarray(front_y), lat_gains.T]
    args += [lat_modes.transpose(1, 2, 0).reshape(chans * chans, modes_x)]
    args += [jnp.asarray(a) for a in (spread8, spread16, spread16.T.copy())]
    args += [depth_modes.reshape(modes_z * chans, chans), depth_local, lat_local, jnp.asarray(back_y)]
    high, low, depth_ops, local_ops, early = exchange(chips, held, tall, block, chans, *args)
    return finish(field, high, low, early, jnp.asarray(back_y), local_ops, depth_ops, chans)


def lead_rows(held, rank):
    lead = LEAD
    while held * (rank + lead) % 16:
        lead += 1
    return lead


def wide_basis(length, modes):
    order = np.arange(modes, dtype=np.float64)[:, None]
    place = np.arange(length, dtype=np.float64)[None, :]
    scales = np.where(order == 0.0, math.sqrt(1.0 / length), math.sqrt(2.0 / length))
    return np.cos(math.pi * order * (place + 0.5) / length) * scales


def shards(field, lat_modes, lat_gains, lat_local, depth_modes, depth_local):
    devices = lax.axis_size("lat")
    rows, _, cells = field.shape
    modes_x, chans, _ = lat_modes.shape
    modes_y, modes_z = lat_gains.shape[0], depth_modes.shape[0]
    args = (field, lat_modes, lat_gains, lat_local, depth_modes, depth_local)
    fits = devices % 2 == 0 and modes_y % (2 * devices) == 0 and modes_y % 64 == 0 and 16 % (modes_y // devices) == 0
    fits = fits and rows % 8 == 0 and cells == 4 * CHUNK and chans * modes_z == 256 and cells == 512 and chans * chans == 256
    if fits:
        held = modes_y // devices
        factors = window_factors(wide_basis(rows * devices, modes_x), devices // 2, 1)
        rank = factors[0].shape[2]
        if rank >= lead_rows(held, rank):
            return shards_chips(devices, factors, *args)
    return shards_rows(*args)


def solution(mesh):
    placed = (P(("group", "lat"), None, None), P(), P(), P(), P(), P())
    return jax.shard_map(
        shards,
        mesh=mesh,
        in_specs=placed,
        out_specs=P(("group", "lat"), None, None),
        check_vma=False,
    )
```

```python
import functools
import math

import jax
import jax.numpy as jnp
import numpy as np
from jax import lax
from jax.experimental import pallas as pl
from jax.experimental.pallas import tpu as pltpu
from jax.sharding import PartitionSpec as P

LINK = jnp.float16
SCALE_OUT = 256.0
SCALE_BACK = 1.0 / 16.0
K0 = math.sqrt(2.0 / math.pi)
K1 = K0 * 0.044715
MIB = 1 << 20


def cosine_basis(length, modes):
    order = np.arange(modes, dtype=np.float64)[:, None]
    place = np.arange(length, dtype=np.float64)[None, :]
    scales = np.where(order == 0.0, math.sqrt(1.0 / length), math.sqrt(2.0 / length))
    return (np.cos(math.pi * order * (place + 0.5) / length) * scales).astype(np.float32)


def halves(x):
    high = jnp.asarray(x).astype(jnp.bfloat16)
    low = (x - high.astype(jnp.float32)).astype(jnp.bfloat16)
    return high, low


def outer_halves(x):
    high = lax.reduce_precision(x, 8, 7)
    return high.astype(jnp.bfloat16), (x - high).astype(jnp.bfloat16)


def np_halves(x):
    high = np.asarray(x, dtype=jnp.bfloat16)
    low = np.asarray(x - high.astype(np.float32), dtype=jnp.bfloat16)
    return high, low


def dot(a, b):
    return jnp.dot(a, b, preferred_element_type=jnp.float32)


def gelu(x):
    half = 0.5 * x
    return half + half * jnp.tanh(x * (K0 + K1 * (x * x)))


def forward_kernel(basis_ref, u_ref, out_ref):
    modes = out_ref.shape[1]

    def body(row, carry):
        both = dot(basis_ref[...], u_ref[row])
        out_ref[row] = (both[:modes] + both[modes:]) * SCALE_OUT
        return carry

    lax.fori_loop(0, u_ref.shape[0], body, 0)


def forward(field, basis, start, rows):
    _, width, cells = field.shape
    modes = basis.shape[0] // 2
    step = math.gcd(rows, 4)
    return pl.pallas_call(
        forward_kernel,
        grid=(rows // step,),
        in_specs=[
            pl.BlockSpec(basis.shape, lambda i: (0, 0)),
            pl.BlockSpec((step, width, cells), lambda i: (i + start // step, 0, 0)),
        ],
        out_specs=pl.BlockSpec((step, modes, cells), lambda i: (i, 0, 0)),
        out_shape=jax.ShapeDtypeStruct((rows, modes, cells), jnp.float32),
        compiler_params=pltpu.CompilerParams(vmem_limit_bytes=40 * MIB),
        cost_estimate=pl.CostEstimate(
            flops=4 * rows * modes * width * cells,
            bytes_accessed=rows * cells * (2 * width + 4 * modes),
            transcendentals=0,
        ),
    )(basis, field)


def middle_kernel(chunks, chans, *refs):
    g_refs = refs[:chunks]
    f_refs = refs[chunks : 2 * chunks]
    b_refs = refs[2 * chunks : 3 * chunks]
    gain_ref, diag_ref = refs[3 * chunks : 3 * chunks + 2]
    out_refs = refs[3 * chunks + 2 :]
    modes = diag_ref.shape[1]
    coef = None
    for g_ref, f_ref in zip(g_refs, f_refs):
        high, low = halves(g_ref[0])
        both = dot(f_ref[...], high)
        part = both[:modes] + both[modes:] + dot(f_ref[:modes], low)
        coef = part if coef is None else coef + part
    coef = coef * gain_ref[0]
    tiles = []
    for lane in range(0, coef.shape[1], 128):
        tile = coef[:, lane : lane + 128]
        total = tile * diag_ref[chans - 1]
        for at in range(2 * chans - 1):
            shift = at - (chans - 1)
            if shift != 0:
                total += pltpu.roll(tile, (-shift) % 128, 1) * diag_ref[at]
        tiles.append(total)
    mixed = jnp.concatenate(tiles, axis=1) if len(tiles) > 1 else tiles[0]
    high, low = halves(mixed)
    stacked = jnp.concatenate([high, low, high], axis=0)
    for b_ref, out_ref in zip(b_refs, out_refs):
        out_ref[0] = dot(b_ref[...], stacked)


def middle(gathered, fronts, backs, gains, diags):
    chunks = len(gathered)
    count, length, width = gathered[0].shape
    modes = diags.shape[1]
    chans = (diags.shape[0] + 1) // 2
    whole = lambda a: pl.BlockSpec(a.shape, lambda i: (0,) * a.ndim)
    block = pl.BlockSpec((1, length, width), lambda i: (i, 0, 0))
    return pl.pallas_call(
        functools.partial(middle_kernel, chunks, chans),
        grid=(count,),
        in_specs=[block] * chunks
        + [whole(a) for a in fronts]
        + [whole(a) for a in backs]
        + [pl.BlockSpec((1, 1, width), lambda i: (i, 0, 0)), whole(diags)],
        out_specs=[block] * chunks,
        out_shape=[jax.ShapeDtypeStruct((count, length, width), jnp.float32)] * chunks,
        compiler_params=pltpu.CompilerParams(vmem_limit_bytes=40 * MIB),
    )(*gathered, *fronts, *backs, gains, diags)


def tail_kernel(piece, u_ref, back_ref, basis_ref, local_ref, depth_ref, *refs):
    out_ref = refs[-1]
    _, width, cells = u_ref.shape
    block = local_ref.shape[1]
    high, low = halves(back_ref[0])
    stacked = jnp.concatenate([high, low, high], axis=0)

    def body(at, carry):
        rows = pl.ds(pl.multiple_of(at * piece, piece), piece)
        u = u_ref[0, rows, :]
        spect = dot(basis_ref[rows, :], stacked)
        parts = []
        for lane in range(0, cells, block):
            tile = u[:, lane : lane + block]
            parts.append(dot(tile, local_ref[0]) + dot(tile, local_ref[1]))
        local = jnp.concatenate(parts, axis=1) if len(parts) > 1 else parts[0]
        first = u.astype(jnp.float32) + gelu(spect + local)
        high1, low1 = halves(first)
        mix = dot(high1, depth_ref[0]) + dot(low1, depth_ref[0]) + dot(high1, depth_ref[1])
        out_ref[0, rows, :] = (first + gelu(mix)).astype(out_ref.dtype)
        return carry

    lax.fori_loop(0, width // piece, body, 0)


def tail(field, back, basis, local, depth, previous, start):
    rows, modes, cells = back.shape
    width = field.shape[1]
    whole = lambda a: pl.BlockSpec(a.shape, lambda i: (0,) * a.ndim)
    operands = [field, back, basis, local, depth]
    specs = [
        pl.BlockSpec((1, width, cells), lambda i: (i + start, 0, 0)),
        pl.BlockSpec((1, modes, cells), lambda i: (i, 0, 0)),
        whole(basis),
        whole(local),
        whole(depth),
    ]
    aliases = {}
    if previous is not None:
        aliases = {len(operands): 0}
        operands.append(previous)
        specs.append(pl.BlockSpec(memory_space=pl.ANY))
    return pl.pallas_call(
        functools.partial(tail_kernel, math.gcd(width, 256)),
        grid=(rows,),
        in_specs=specs,
        out_specs=pl.BlockSpec((1, width, cells), lambda i: (i + start, 0, 0)),
        out_shape=jax.ShapeDtypeStruct(field.shape, jnp.bfloat16),
        input_output_aliases=aliases,
        compiler_params=pltpu.CompilerParams(vmem_limit_bytes=48 * MIB),
        cost_estimate=pl.CostEstimate(
            flops=2 * rows * width * cells * (4 * cells),
            bytes_accessed=4 * rows * width * cells,
            transcendentals=2 * rows * width * cells,
        ),
    )(*operands)


def block_diagonal(small, size):
    chans = small.shape[0]
    copies = size // chans
    ids = np.arange(size) // chans
    mask = (ids[:, None] == ids[None, :]).astype(np.float32)
    return jnp.tile(small, (copies, copies)) * mask


def shards_rows(field, lat_modes, lat_gains, lat_local, depth_modes, depth_local):
    highest = lax.Precision.HIGHEST
    devices = lax.axis_size("lat")
    rows_dev, width_y, cells = field.shape
    modes_x, chans, _ = lat_modes.shape
    modes_y = lat_gains.shape[0]
    modes_z = depth_modes.shape[0]
    depth = cells // chans
    width_x = rows_dev * devices
    chunks = 2 if rows_dev % 16 == 0 else 1
    rows = rows_dev // chunks
    splits = max(1, devices // modes_y)
    held = modes_y * splits // devices
    span = cells // splits
    basis_x = cosine_basis(width_x, modes_x)
    basis_y = cosine_basis(width_y, modes_y)
    basis_z = cosine_basis(depth, modes_z)

    high_y, low_y = np_halves(basis_y)
    front_y = jnp.asarray(np.concatenate([high_y, low_y], axis=0))
    back_y = jnp.asarray(np.concatenate([high_y, high_y, low_y], axis=0).T.copy())
    fronts, backs = [], []
    for chunk in range(chunks):
        part = basis_x.reshape(modes_x, devices, chunks, rows)[:, :, chunk].reshape(modes_x, -1)
        high_x, low_x = np_halves(part)
        fronts.append(jnp.asarray(np.concatenate([high_x, low_x], axis=0)))
        backs.append(jnp.asarray(np.concatenate([high_x, high_x, low_x], axis=0).T.copy()))

    gathered = []
    for chunk in range(chunks):
        coef_y = forward(field, front_y, chunk * rows, rows)
        sent = coef_y.astype(LINK).reshape(rows, modes_y, splits, span)
        sent = sent.transpose(1, 2, 0, 3).reshape(modes_y * splits, rows, span)
        gathered.append(lax.all_to_all(sent, "lat", split_axis=0, concat_axis=0, tiled=True))

    shift = np.arange(2 * chans - 1)[:, None, None] - (chans - 1)
    places = np.arange(chans)
    pick = (places[None, :, None] == places[None, None, :] + shift).astype(np.float32)
    diags = jnp.sum(lat_modes[None] * pick[:, None], axis=2)
    diags = jnp.tile(diags, (1, 1, 128 // chans))
    me = lax.axis_index("lat")
    gain_rows = lax.dynamic_slice_in_dim(lat_gains, me * held // splits, held, 0)
    gain_rows = jnp.tile(gain_rows * (SCALE_BACK / SCALE_OUT), (1, span // chans))[:, None, :]

    spread = np.kron(basis_z.T, np.eye(chans, dtype=np.float32))
    ids = np.arange(modes_z * chans) // chans
    mask = (ids[:, None] == ids[None, :]).astype(np.float32)
    mixers = jnp.tile(depth_modes.reshape(modes_z * chans, chans), (1, modes_z)) * mask
    inner = jnp.dot(mixers, spread.T, precision=highest)
    whole = jnp.dot(spread, inner, precision=highest) + block_diagonal(depth_local, cells)
    depth_pair = jnp.stack(outer_halves(whole))
    local_pair = jnp.stack(outer_halves(block_diagonal(lat_local, math.gcd(cells, 256))))

    received = []
    for got in gathered:
        got = got.reshape(devices, held, rows, span).transpose(1, 0, 2, 3).astype(jnp.float32)
        received.append(got.reshape(held, devices * rows, span))
    mixed = middle(received, fronts, backs, gain_rows, diags)
    returned = []
    for part in mixed:
        part = part.astype(LINK).reshape(held, devices, rows, span).transpose(1, 0, 2, 3)
        part = part.reshape(devices * held, rows, span)
        returned.append(lax.all_to_all(part, "lat", split_axis=0, concat_axis=0, tiled=True))
    out = None
    for chunk, part in enumerate(returned):
        part = part.reshape(modes_y, splits, rows, span).transpose(2, 0, 1, 3)
        part = part.reshape(rows, modes_y, cells).astype(jnp.float32) * (1.0 / SCALE_BACK)
        out = tail(field, part, back_y, local_pair, depth_pair, out, chunk * rows)
    return out

LINK_OUT = 64.0
LINK_BACK = 1.0 / 32.0
C0 = 2.0 * K0
C1 = 8.0 * K1


def act(h):
    return h + h * jnp.tanh(h * (C0 + C1 * (h * h)))


def window_factors(basis, windows, fine):
    modes = basis.shape[0]
    blocks = basis.reshape(modes, windows, -1).transpose(1, 0, 2)
    left, sizes, right = np.linalg.svd(blocks, full_matrices=False)
    left = left * sizes[:, None, :]
    top = np.abs(basis).max()
    rank = fine
    while rank < sizes.shape[1]:
        product = left[:, :, :rank] @ right[:, :rank]
        if np.abs(product - blocks).max() <= 2.0 ** -23 * top:
            break
        rank += fine
    return left[:, :, :rank], right[:, :rank]


def turn(x, unit):
    place = lax.broadcasted_iota(jnp.int32, (x.shape[0], 128), 1)
    place = (128 - unit - place // unit * unit) + place % unit
    tiles = [jnp.take_along_axis(x[:, at : at + 128], place, axis=1) for at in range(0, x.shape[1], 128)]
    return jnp.concatenate(tiles[::-1], axis=1)


LEAD = 9
CHUNK = 128
ORDER = (0, 3, 1, 2)
EARLY = 4


def exact(a, b):
    return jnp.dot(a, b, preferred_element_type=jnp.float32, precision=lax.Precision.HIGHEST)


def turned_dot(a, b, precision=None):
    return lax.dot_general(a, b, (((0,), (0,)), ((), ())), precision=precision, preferred_element_type=jnp.float32)


def quarter_mask(size, unit):
    half = size // unit // 2
    row = lax.broadcasted_iota(jnp.int32, (size, size), 0) // unit
    lane = lax.broadcasted_iota(jnp.int32, (size, size), 1) // unit
    return (row == jnp.where(lane < half, lane, 3 * half - 1 - lane)).astype(jnp.float32)


def block_mask(size, unit, flip):
    row = lax.broadcasted_iota(jnp.int32, (size, size), 0) // unit
    lane = lax.broadcasted_iota(jnp.int32, (size, size), 1) // unit
    return (row == (size // unit - 1 - lane if flip else lane)).astype(jnp.float32)


def exchange_kernel(chips, held, tall, chans, *refs):
    field, press_all, grow_all, front_in, back_in, picks_in, folds_in, folds_t_in, sides_in = refs[:9]
    basis, gains, modes_in, spread8, spread16, spread_t, depth_in, depth_local, lat_local, synth = refs[9:19]
    high_out, low_out, depth_out, local_out, early_out = refs[19:24]
    (u, highs, lows, part, fresh, send, land, reply, home, wide_high, wide_low, diags, depth_ops, local_ops, firsts, rhs) = refs[24:40]
    press, grow, front, back, picks, folds, folds_t, sides = refs[40:48]
    load_sem, table_sem, pair_send, pair_recv, out_send, out_recv, in_send, in_recv, hand_send, hand_recv, store_sem, ops_sem, again_sem, early_sem = refs[48:]
    rows, width, cells = field.shape
    modes = basis.shape[0] // 2
    chunks = cells // CHUNK
    block = send.shape[2]
    mesh_ids = pl.DeviceIdType.MESH
    me = lax.axis_index("lat")
    chip, core = me // 2, lax.rem(me, 2)
    other = chip * 2 + 1 - core
    subs = 4
    span = rows // subs

    def load(ch, sub):
        take = pl.ds(sub * span, span)
        return pltpu.make_async_copy(
            field.at[take, :, pl.ds(ORDER[ch] * CHUNK, CHUNK)], u.at[ch % 2, take], load_sem.at[ch, sub]
        )

    def tables():
        sources = (press_all.at[me], grow_all.at[me], front_in, back_in, picks_in, folds_in, folds_t_in, sides_in)
        targets = (press, grow, front, back, picks, folds, folds_t, sides)
        pairs = enumerate(zip(sources, targets))
        return [pltpu.make_async_copy(source, target, table_sem.at[k]) for k, (source, target) in pairs]

    for sub in range(subs):
        load(0, sub).start()
    tables()[0].start()
    for sub in range(subs):
        load(1, sub).start()
    for copy in tables()[1:]:
        copy.start()

    barrier = pltpu.get_barrier_semaphore()
    for off in range(1, chips):
        peer = lax.rem(chip + off, chips) * 2 + core
        pl.semaphore_signal(barrier, inc=1, device_id={"lat": peer}, device_id_type=mesh_ids)
    pl.semaphore_signal(barrier, inc=1, device_id={"lat": other}, device_id_type=mesh_ids)

    def pair_copy(ch):
        return pltpu.make_async_remote_copy(
            src_ref=part.at[ch, 1 - core],
            dst_ref=fresh.at[ch],
            send_sem=pair_send.at[ch],
            recv_sem=pair_recv.at[ch],
            device_id={"lat": other},
            device_id_type=mesh_ids,
        )

    def chip_copy(source, target, send_sems, recv_sems, ch, off):
        to = lax.rem(chip + off, chips)
        return pltpu.make_async_remote_copy(
            src_ref=source.at[ch, to],
            dst_ref=target.at[chip],
            send_sem=send_sems.at[ch, off - 1],
            recv_sem=recv_sems.at[ch, off - 1],
            device_id={"lat": to * 2 + core},
            device_id_type=mesh_ids,
        )

    def out_copy(ch, off):
        return chip_copy(send, land.at[ch], out_send, out_recv, ch, off)

    def in_copy(ch, off):
        return chip_copy(reply, home.at[ch, core], in_send, in_recv, ch, off)

    def hand_copy(ch, off):
        slot = lax.rem(chip + chips - off, chips)
        return pltpu.make_async_remote_copy(
            src_ref=home.at[ch, core, slot],
            dst_ref=home.at[ch, core, slot],
            send_sem=hand_send.at[ch, off],
            recv_sem=hand_recv.at[ch, off],
            device_id={"lat": other},
            device_id_type=mesh_ids,
        )

    def analyse(ch):
        for sub in range(subs):
            load(ch, sub).wait()

            def body(k, carry):
                x = sub * span + 2 * k
                pair = jnp.concatenate([u[ch % 2, x], u[ch % 2, x + 1]], axis=1)
                both = dot(basis[...], pair)
                high, low = halves(both[:modes] + both[modes:])
                for at in range(2):
                    highs[x + at] = high[:, at * CHUNK : (at + 1) * CHUNK]
                    lows[x + at] = low[:, at * CHUNK : (at + 1) * CHUNK]
                return carry

            lax.fori_loop(0, span // 2, body, 0, unroll=True)
        if ch + 2 < chunks:
            for sub in range(subs):
                load(ch + 2, sub).start()
        if ch == 0:
            tables()[0].wait()
        count = press.shape[0]
        for group in range(0, modes // 16, 2):
            stacks = []
            for g in (group, group + 1):
                take = slice(16 * g, 16 * g + 16)
                high = highs[:, take, :].reshape(rows * 16, CHUNK)
                low = lows[:, take, :].reshape(rows * 16, CHUNK)
                stacks.append(jnp.concatenate([high, low, high], axis=0))
            product = dot(press[...], jnp.concatenate(stacks, axis=1))
            half, within = divmod(group, modes // 32)
            for at in range(2):
                part[ch, half, count * (within + at) : count * (within + at + 1), :] = product[:, at * CHUNK : (at + 1) * CHUNK]

    def spill(value, target, ch):
        high, low = halves(value)
        place = lax.broadcasted_iota(jnp.int32, value.shape, 0) % block
        target[ch] = jnp.where(place < tall, high, low).reshape(chips, block, CHUNK)

    def emit(ch):
        pair_copy(ch).wait_recv()
        spill(part[ch, core] + fresh[ch], send, ch)
        for off in range(1, chips):
            out_copy(ch, off).start()
        land[ch, chip] = send[ch, chip]

    def mixers():
        rest, total = modes_in[...], None
        for _ in range(3):
            term = rest.astype(jnp.bfloat16)
            rest = rest - term.astype(jnp.float32)
            product = turned_dot(term, picks[...])
            total = product if total is None else total + product
        for at in range(2 * chans - 1):
            diags[at] = total[:, at * 128 : (at + 1) * 128]

    def prepare():
        half = folds.shape[1]
        local = exact(exact(spread_t[...], depth_local[...]), spread16[...]) * block_mask(half, chans, False)
        for side in range(2):
            mixer = exact(exact(sides[side], depth_in[...]), spread8[...]) * block_mask(folds.shape[2], chans, False)
            whole = 0.5 * exact(exact(folds[side], mixer), folds_t[side]) + 0.25 * local
            high, low = halves(whole)
            for at, x in enumerate((high, high, low)):
                depth_ops[side, at * half : (at + 1) * half, :] = x
        spot = exact(exact(spread_t[...], lat_local[...]), spread16[...]) * 0.5
        high, low = halves(spot * quarter_mask(half, chans))
        local_ops[:half, :] = high
        local_ops[half:, :] = low
        for slot in range(EARLY):
            rhs[slot, 4 * modes : 4 * modes + half, :] = high
            rhs[slot, 4 * modes + half :, :] = low

    def ops_copies():
        return (
            pltpu.make_async_copy(depth_ops, depth_out, ops_sem.at[0]),
            pltpu.make_async_copy(local_ops, local_out, ops_sem.at[1]),
        )

    first_q = core * (modes // 2) + chip * held

    def blend(ch):
        for off in range(1, chips):
            out_copy(ch, off).wait_recv()
        values = land[ch].reshape(chips * block, CHUNK)
        coef = dot(front[...], jnp.concatenate([values, values], axis=0))
        scale = turned_dot(gains[...], spread8[...], lax.Precision.HIGHEST)
        size = diags.shape[1]
        upper, lower = [], []
        for q in range(held):
            tile = coef[q * size : (q + 1) * size] * gains_row(scale, q)
            total = tile * diags[chans - 1]
            for at in range(2 * chans - 1):
                shift = at - (chans - 1)
                if shift != 0:
                    total += pltpu.roll(tile, (-shift) % 128, 1) * diags[at]
            if 2 * ORDER[ch] >= chunks:
                total = turn(total, chans)
            high, low = halves(total)
            upper.append(high)
            lower.append(low)
        spill(dot(back[...], jnp.concatenate(upper + lower + upper, axis=0)), reply, ch)
        for off in range(1, chips):
            in_copy(ch, off).start()
        home[ch, core, chip] = reply[ch, chip]
        hand_copy(ch, 0).start()

    def gains_row(scale, q):
        at = lax.broadcasted_iota(jnp.int32, scale.shape, 0)
        return jnp.sum(jnp.where(at == first_q + q, scale, 0.0), axis=0, keepdims=True)

    def hand(ch):
        for off in range(1, chips):
            in_copy(ch, off).wait_recv()
            hand_copy(ch, off).start()

    def store_copies(ch):
        lanes = pl.ds((ch - 2) * CHUNK, CHUNK)
        return (
            pltpu.make_async_copy(wide_high.at[ch], high_out.at[:, :, lanes], store_sem.at[ch - 2, 0]),
            pltpu.make_async_copy(wide_low.at[ch], low_out.at[:, :, lanes], store_sem.at[ch - 2, 1]),
        )

    def again(ch):
        return pltpu.make_async_copy(field.at[:, :, pl.ds(ORDER[ch] * CHUNK, CHUNK)], u.at[ch], again_sem.at[ch])

    def early_copy(x, slot):
        return pltpu.make_async_copy(firsts.at[slot], early_out.at[x], early_sem.at[slot])

    def early(start, stop):
        def draw(x, slot):
            high = jnp.concatenate([wide_high[0, x], wide_high[1, x]], axis=1)
            low = jnp.concatenate([wide_low[0, x], wide_low[1, x]], axis=1)
            for at, part_rows in enumerate((high, low, high, low)):
                rhs[slot, at * modes : (at + 1) * modes, :] = part_rows
            both = jnp.concatenate([u[0, x], u[1, x]], axis=1)
            return both, dot(jnp.concatenate([synth[...], both, both], axis=1), rhs[slot])

        def body(k, carry):
            @pl.when(k > 0)
            def _():
                for slot in range(EARLY):
                    early_copy(EARLY * (k - 1) + slot, slot).wait()

            drawn = [draw(EARLY * k, 0)]
            for slot in range(EARLY):
                if slot + 1 < EARLY:
                    drawn.append(draw(EARLY * k + slot + 1, slot + 1))
                both, h = drawn[slot]
                wide = both.astype(jnp.float32)
                firsts[slot, :, :CHUNK] = wide[:, :CHUNK] + act(h[:, :CHUNK])
                firsts[slot, :, CHUNK:] = turn(wide[:, CHUNK:], chans) + act(h[:, CHUNK:])
            for slot in range(EARLY):
                early_copy(EARLY * k + slot, slot).start()
            return carry

        lax.fori_loop(start // EARLY, stop // EARLY, body, 0)

    def expand(ch):
        for off in range(chips):
            hand_copy(ch, off).wait_recv()
        each = 16 // held
        for group in range(0, modes // 16, 2):
            stacks = []
            for g in (group, group + 1):
                half, within = divmod(g, modes // 32)
                take = slice(each * within, each * (within + 1))
                values = home[ch, half, take].reshape(each * block, CHUNK)
                stacks.append(jnp.concatenate([values, values], axis=0))
            high, low = halves(dot(grow[...], jnp.concatenate(stacks, axis=1)))
            for at in range(2):
                take = slice(16 * (group + at), 16 * (group + at + 1))
                lanes = slice(at * CHUNK, (at + 1) * CHUNK)
                wide_high[ch, :, take, :] = high[:, lanes].reshape(rows, 16, CHUNK)
                wide_low[ch, :, take, :] = low[:, lanes].reshape(rows, 16, CHUNK)
        if ch >= 2:
            for copy in store_copies(ch):
                copy.start()

    analyse(0)
    pl.semaphore_wait(barrier, chips)
    pair_copy(0).start()
    emit(0)
    analyse(1)
    pair_copy(1).start()
    for copy in tables()[1:]:
        copy.wait()
    mixers()
    emit(1)
    analyse(2)
    pair_copy(2).start()
    blend(0)
    analyse(3)
    pair_copy(3).start()
    again(0).start()
    again(1).start()
    blend(1)
    emit(2)
    emit(3)
    prepare()
    for copy in ops_copies():
        copy.start()
    hand(0)
    hand(1)
    expand(0)
    expand(1)
    again(0).wait()
    again(1).wait()
    quarter = rows // 4
    early(0, quarter)
    blend(2)
    early(quarter, 2 * quarter)
    blend(3)
    early(2 * quarter, 3 * quarter)
    hand(2)
    early(3 * quarter, rows)
    hand(3)
    expand(2)
    expand(3)
    for slot in range(EARLY):
        early_copy(rows - EARLY + slot, slot).wait()
    for ch in range(chunks):
        pair_copy(ch).wait_send()
        for off in range(1, chips):
            out_copy(ch, off).wait_send()
            in_copy(ch, off).wait_send()
        for off in range(chips):
            hand_copy(ch, off).wait_send()
    for ch in range(2, chunks):
        for copy in store_copies(ch):
            copy.wait()
    for copy in ops_copies():
        copy.wait()


def exchange(chips, held, tall, block, chans, *args):
    field, press_all, grow_all = args[:3]
    basis, gains = args[9:11]
    rows, width, cells = field.shape
    modes = basis.shape[0] // 2
    chunks = cells // CHUNK
    half = cells // 2
    size = args[11].shape[1]
    hbm = pl.BlockSpec(memory_space=pl.ANY)
    whole = lambda a: pl.BlockSpec(a.shape, lambda: (0,) * a.ndim)
    dma = pltpu.SemaphoreType.DMA
    bf16, f32 = jnp.bfloat16, jnp.float32
    blocks = (chunks, chips, block, CHUNK)
    return pl.pallas_call(
        functools.partial(exchange_kernel, chips, held, tall, chans),
        in_specs=[hbm] * 9 + [whole(a) for a in args[9:]],
        out_specs=[hbm] * 5,
        out_shape=[
            jax.ShapeDtypeStruct((rows, modes, half), bf16),
            jax.ShapeDtypeStruct((rows, modes, half), bf16),
            jax.ShapeDtypeStruct((2, 3 * half, half), bf16),
            jax.ShapeDtypeStruct((2 * half, half), bf16),
            jax.ShapeDtypeStruct((rows, width, half), f32),
        ],
        scratch_shapes=[
            pltpu.VMEM((2, rows, width, CHUNK), bf16),
            pltpu.VMEM((rows, modes, CHUNK), bf16),
            pltpu.VMEM((rows, modes, CHUNK), bf16),
            pltpu.VMEM((chunks, 2, chips * block, CHUNK), f32),
            pltpu.VMEM((chunks, chips * block, CHUNK), f32),
            pltpu.VMEM(blocks, bf16),
            pltpu.VMEM(blocks, bf16),
            pltpu.VMEM(blocks, bf16),
            pltpu.VMEM((chunks, 2) + blocks[1:], bf16),
            pltpu.VMEM((chunks, rows, modes, CHUNK), bf16),
            pltpu.VMEM((chunks, rows, modes, CHUNK), bf16),
            pltpu.VMEM((2 * chans - 1, size, 128), f32),
            pltpu.VMEM((2, 3 * half, half), bf16),
            pltpu.VMEM((2 * half, half), bf16),
            pltpu.VMEM((EARLY, width, half), f32),
            pltpu.VMEM((EARLY, 4 * modes + 2 * half, half), bf16),
            pltpu.VMEM(press_all.shape[1:], bf16),
            pltpu.VMEM(grow_all.shape[1:], bf16),
            *[pltpu.VMEM(a.shape, a.dtype) for a in args[3:9]],
            dma((chunks, 4)),
            dma((8,)),
            dma((chunks,)),
            dma((chunks,)),
            dma((chunks, chips - 1)),
            dma((chunks, chips - 1)),
            dma((chunks, chips - 1)),
            dma((chunks, chips - 1)),
            dma((chunks, chips)),
            dma((chunks, chips)),
            dma((2, 2)),
            dma((2,)),
            dma((2,)),
            dma((EARLY,)),
        ],
        compiler_params=pltpu.CompilerParams(collective_id=5, has_side_effects=True, vmem_limit_bytes=58 * MIB),
    )(*args)


def finish_kernel(chans, u_ref, high_ref, low_ref, early_ref, basis_ref, local_ref, depth_ref, out_ref, *rhs):
    rows, width, cells = u_ref.shape
    half = cells // 2
    modes = high_ref.shape[1]

    @pl.when(pl.program_id(0) == 0)
    def _():
        for r in rhs:
            r[4 * modes :, :] = local_ref[...]

    def first_layer(row):
        high, low = high_ref[row], low_ref[row]
        for k, x in enumerate((high, low, high, low)):
            rhs[row][modes * k : modes * (k + 1), :] = x
        u = u_ref[row, :, CHUNK : CHUNK + half]
        h = dot(jnp.concatenate([basis_ref[...], u, u], axis=1), rhs[row][...])
        wide = u.astype(jnp.float32)
        lower = wide[:, :CHUNK] + act(h[:, :CHUNK])
        upper = turn(wide[:, CHUNK:], chans) + act(h[:, CHUNK:])
        return [
            jnp.concatenate([early_ref[row, :, :CHUNK], lower], axis=1),
            jnp.concatenate([early_ref[row, :, CHUNK:], upper], axis=1),
        ]

    def second_layer(row, first):
        mixes = []
        for side, x in enumerate((first[0] + first[1], first[0] - first[1])):
            high, low = halves(x)
            mixes.append(dot(jnp.concatenate([high, low, high], axis=1), depth_ref[side]))
        upper = first[1] + act(mixes[0] - mixes[1])
        out_ref[row, :, :half] = (first[0] + act(mixes[0] + mixes[1])).astype(out_ref.dtype)
        out_ref[row, :, half:] = turn(upper, chans).astype(out_ref.dtype)

    firsts = [first_layer(0)]
    for row in range(rows):
        if row + 1 < rows:
            firsts.append(first_layer(row + 1))
        second_layer(row, firsts[row])


def finish(field, high, low, early, basis, local, depth, chans):
    rows, width, cells = field.shape
    modes = high.shape[1]
    step = math.gcd(rows, 4)
    whole = lambda a: pl.BlockSpec(a.shape, lambda i: (0,) * a.ndim)
    block = pl.BlockSpec((step, width, cells), lambda i: (i, 0, 0))
    thin = pl.BlockSpec((step, modes, cells // 2), lambda i: (i, 0, 0))
    wide = pl.BlockSpec((step, width, cells // 2), lambda i: (i, 0, 0))
    return pl.pallas_call(
        functools.partial(finish_kernel, chans),
        grid=(rows // step,),
        in_specs=[block, thin, thin, wide, whole(basis), whole(local), whole(depth)],
        out_specs=block,
        out_shape=jax.ShapeDtypeStruct(field.shape, jnp.bfloat16),
        scratch_shapes=[pltpu.VMEM((4 * modes + cells, cells // 2), jnp.bfloat16)] * step,
        compiler_params=pltpu.CompilerParams(vmem_limit_bytes=56 * MIB),
        cost_estimate=pl.CostEstimate(
            flops=2 * rows * width * cells * (3 * cells),
            bytes_accessed=4 * rows * width * cells,
            transcendentals=2 * rows * width * cells,
        ),
    )(field, high, low, early, basis, local, depth)


def stack_halves(x, order, axis):
    pair = np_halves(np.asarray(x, dtype=np.float32))
    return np.concatenate([pair[k] for k in order], axis=axis)


def shards_chips(devices, factors, field, lat_modes, lat_gains, lat_local, depth_modes, depth_local):
    rows, width_y, cells = field.shape
    modes_x, chans, _ = lat_modes.shape
    modes_y = lat_gains.shape[0]
    modes_z = depth_modes.shape[0]
    depth = cells // chans
    chips = devices // 2
    held = modes_y // devices
    basis_y = cosine_basis(width_y, modes_y)
    basis_z = cosine_basis(depth, modes_z)
    left, right = factors
    rank = left.shape[2]
    lead = lead_rows(held, rank)
    tall, block, each = held * rank, held * (rank + lead), 16 // held

    slots = [q * rank + j for q in range(held) for j in range(rank)]
    slots = np.array(slots + [q * rank + j for q in range(held) for j in range(lead)])
    full = (np.arange(block) < tall).astype(np.float32)

    own = right.reshape(chips, rank, 2, rows).transpose(0, 2, 1, 3).reshape(devices, rank, rows)
    kron = np.einsum("djx,qr->dqjxr", own, np.eye(16)).reshape(devices, each, tall, rows * 16)
    kron = kron[:, :, slots].reshape(devices, each * block, rows * 16)
    press = stack_halves(kron, (0, 0, 1), 2)
    high, low = np_halves(np.float32(0.5 * kron.transpose(0, 2, 1)))
    low = (low.astype(np.float32) * np.tile(full, each)).astype(jnp.bfloat16)
    grow = np.concatenate([high, low], axis=2)

    sides = np.einsum("ipj,qr->qpirj", left, np.eye(held)).reshape(held * modes_x, chips, tall)
    flat = np.float32(sides[:, :, slots].reshape(held * modes_x, chips * block))
    high, low = np_halves(flat)
    low = (low.astype(np.float32) * np.tile(full, chips)).astype(jnp.bfloat16)
    front = np.concatenate([high, low], axis=1)
    back = stack_halves(flat.T, (0, 0, 1), 1)
    front_y = stack_halves(basis_y, (0, 1), 0)
    back_y = stack_halves(basis_y.T, (0, 0, 1, 1), 1)

    places = np.arange(chans)
    shift = np.arange(2 * chans - 1) - (chans - 1)
    pick = (places[:, None, None, None] == (places[None, None, None, :] + shift[None, None, :, None])) & (
        places[None, :, None, None] == places[None, None, None, :]
    )
    picks = np.tile(pick.reshape(chans * chans, 2 * chans - 1, chans), (1, 1, 128 // chans))
    picks = picks.reshape(chans * chans, -1).astype(jnp.bfloat16)

    half = depth // 2
    folds = np.stack([np.kron(basis_z[side::2, :half].T, np.eye(chans)) for side in range(2)]).astype(np.float32)
    kinds = np.eye(modes_z)
    sides_z = np.stack([np.kron(kinds[side::2], np.eye(chans)) for side in range(2)]).astype(np.float32)
    spread8 = np.tile(np.eye(chans, dtype=np.float32), (1, modes_z // 2))
    spread16 = np.tile(np.eye(chans, dtype=np.float32), (1, half))

    tables = [press, grow, front, back, picks, folds, folds.transpose(0, 2, 1).copy(), sides_z]
    args = [field] + [jnp.asarray(a) for a in tables] + [jnp.asarray(front_y), lat_gains.T]
    args += [lat_modes.transpose(1, 2, 0).reshape(chans * chans, modes_x)]
    args += [jnp.asarray(a) for a in (spread8, spread16, spread16.T.copy())]
    args += [depth_modes.reshape(modes_z * chans, chans), depth_local, lat_local, jnp.asarray(back_y)]
    high, low, depth_ops, local_ops, early = exchange(chips, held, tall, block, chans, *args)
    return finish(field, high, low, early, jnp.asarray(back_y), local_ops, depth_ops, chans)


def lead_rows(held, rank):
    lead = LEAD
    while held * (rank + lead) % 16:
        lead += 1
    return lead


def wide_basis(length, modes):
    order = np.arange(modes, dtype=np.float64)[:, None]
    place = np.arange(length, dtype=np.float64)[None, :]
    scales = np.where(order == 0.0, math.sqrt(1.0 / length), math.sqrt(2.0 / length))
    return np.cos(math.pi * order * (place + 0.5) / length) * scales


def shards(field, lat_modes, lat_gains, lat_local, depth_modes, depth_local):
    devices = lax.axis_size("lat")
    rows, _, cells = field.shape
    modes_x, chans, _ = lat_modes.shape
    modes_y, modes_z = lat_gains.shape[0], depth_modes.shape[0]
    args = (field, lat_modes, lat_gains, lat_local, depth_modes, depth_local)
    fits = devices % 2 == 0 and modes_y % (2 * devices) == 0 and modes_y % 64 == 0 and 16 % (modes_y // devices) == 0
    fits = fits and rows % (4 * EARLY) == 0 and cells == 4 * CHUNK and chans * modes_z == 256 and cells == 512 and chans * chans == 256
    if fits:
        held = modes_y // devices
        factors = window_factors(wide_basis(rows * devices, modes_x), devices // 2, 1)
        rank = factors[0].shape[2]
        if rank >= lead_rows(held, rank):
            return shards_chips(devices, factors, *args)
    return shards_rows(*args)


def solution(mesh):
    placed = (P(("group", "lat"), None, None), P(), P(), P(), P(), P())
    return jax.shard_map(
        shards,
        mesh=mesh,
        in_specs=placed,
        out_specs=P(("group", "lat"), None, None),
        check_vma=False,
    )
```
